32 devices in a mesh: groups: 2 (over y), seq: 4 (over z), tensor: 4 (over x, core).
Axes of the slice: x: 2, y: 2, z: 4, core: 2. Of those that a mesh axis runs over, the one named last changes fastest.
Arguments:
- video_states: bfloat16 [3072, 5120], P(('groups', 'seq'), 'tensor'), parts along dimension 0, may hold values from -16 to 16
- query_self: bfloat16 [3072, 3072], P(('groups', 'seq'), 'tensor'), parts along dimension 0, may hold values from -4.5 to 4.5
- key_self: bfloat16 [3072, 3072], P(('groups', 'seq'), 'tensor'), parts along dimension 0, may hold values from -4.5 to 4.5
- value_self: bfloat16 [3072, 3072], P(('groups', 'seq'), 'tensor'), parts along dimension 0, may hold values from -4.5 to 4.5
- out_weight: bfloat16 [3072, 5120], P('tensor'), may hold values from -0.109375 to 0.109375
- cross_gain: float32 [5120], P('tensor'), may hold values from 0.1 to 1.9
- query_weight: bfloat16 [5120, 3072], P(None, 'tensor'), may hold values from -0.15625 to 0.15625
- text_memory: bfloat16 [1024, 4096], P('groups', 'seq'), parts along dimension 0, may hold values from -16 to 16
- text_gain: float32 [4096], P('seq'), may hold values from 0.1 to 1.9
- text_weight: bfloat16 [4096, 2, 3072], P('seq', None, 'tensor'), may hold values from -0.09375 to 0.09375
- prompt_length: int32 [2], P('groups'), parts along dimension 0, may hold values from 64 to 512
Outputs:
- residual_out: bfloat16 [3072, 5120], P(('groups', 'seq'), 'tensor'), parts along dimension 0
- cross_out: bfloat16 [3072, 3072], P(('groups', 'seq'), 'tensor'), parts along dimension 0
The draws below stay inside these ranges and needn't reach their ends.
There are 2 independent parts, one for each index of `groups`. The reference program is written for one: setup_inputs(seed, part) draws one part's arguments, and reference() takes and returns one part's arrays. A program takes and returns all parts, laid end to end along the dimension named above; an argument that names none is the same for every part. Nothing has to cross between parts.
All inputs are finite; a program needn't handle non-finite values.
Results may differ from the reference program's by a relative error of at most 0.019.
Values may be sent and summed in bfloat16 or wider, within the bound.
No kernel may reach another device: no remote copies, remote signals or barrier semaphores. Data moves between devices by JAX's collectives and lax.ppermute only.
A program may use at most 128 MiB of HBM per device.

```python
import math
import jax
import jax.numpy as jnp
from jax import lax

D = 5120
DT = 4096
HD = 128
TXT = 512
HEADS = 24
HC = 3072
TOKENS = 1536


def scaled_field(key, row_count, col_count):
    first, second, third = jax.random.split(key, 3)
    base = jax.random.normal(first, (row_count, col_count), jnp.float32)
    col_pos = jnp.arange(col_count, dtype=jnp.float32) / col_count
    row_scale = jnp.exp(jax.random.uniform(second, (row_count, 1), jnp.float32, math.log(0.7), math.log(1.4)))
    col_scale = jnp.exp(jax.random.uniform(third, (col_count,), jnp.float32, math.log(0.7), math.log(1.4))) * jnp.exp(col_pos * math.log(3.0))
    return base * row_scale * col_scale


def draw_video_states(key, part):
    field = scaled_field(jax.random.fold_in(key, 3), TOKENS, D)
    return jnp.clip(0.3 * field, -16.0, 16.0).astype(jnp.bfloat16)


def draw_text_memory(key, part):
    field = scaled_field(jax.random.fold_in(key, 5), TXT, DT)
    return jnp.clip(field, -16.0, 16.0).astype(jnp.bfloat16)


def attention_pair(key):
    first, second = jax.random.split(jax.random.fold_in(key, 7))
    queries = jnp.clip(1.5 * jax.random.normal(first, (TOKENS, HC), jnp.float32), -4.5, 4.5)
    keyrows = jnp.clip(1.5 * jax.random.normal(second, (TOKENS, HC), jnp.float32), -4.5, 4.5)
    return (queries, keyrows)


def draw_query_self(key, part):
    queries, keyrows = attention_pair(key)
    return queries.astype(jnp.bfloat16)


def draw_key_self(key, part):
    queries, keyrows = attention_pair(key)
    return keyrows.astype(jnp.bfloat16)


def levels(rng, dims, shards, smallest, largest):
    gain = 1.0
    for position, blocks in shards:
        heights = jax.random.uniform(jax.random.fold_in(jax.random.fold_in(rng, 6), position), (blocks,), jnp.float32, smallest / len(shards), largest / len(shards))
        gain = gain * jnp.repeat(jnp.exp(heights), dims[position] // blocks).reshape((-1,) + (1,) * (len(dims) - 1 - position))
    return gain


def gaussian(own_key, shape, scale, most, cuts=(), kind=jnp.bfloat16):
    factor_of = levels(own_key, shape, cuts, -0.22, 0.18) if cuts else 1.0
    array = jax.random.normal(own_key, shape, jnp.float32) * scale * factor_of
    return jnp.minimum(jnp.maximum(array, -most), most).astype(kind)


def setup_inputs(seed: int = 0, part: int = 0) -> dict:
    splits = jax.random.split(jax.random.key(seed), 12)
    part_splits = jax.random.split(jax.random.fold_in(splits[11], part), 12)
    return {
        "video_states": draw_video_states(jax.random.fold_in(jax.random.fold_in(splits[11], part), 71), part),
        "query_self": draw_query_self(jax.random.fold_in(jax.random.fold_in(splits[11], part), 71), part),
        "key_self": draw_key_self(jax.random.fold_in(jax.random.fold_in(splits[11], part), 71), part),
        "value_self": gaussian(part_splits[3], (TOKENS, HC), 1.0, 4.5, ((0, 4), (1, 4))),
        "out_weight": gaussian(splits[4], (HC, D), HC ** -0.5, 0.109375, ((0, 4),)),
        "cross_gain": jnp.clip(1.0 + 0.18 * jax.random.normal(splits[5], (D,), jnp.float32), 0.1, 1.9),
        "query_weight": gaussian(splits[6], (D, HC), (D // 4) ** -0.5, 0.15625, ((1, 4),)),
        "text_memory": draw_text_memory(jax.random.fold_in(jax.random.fold_in(splits[11], part), 71), part),
        "text_gain": jnp.clip(1.0 + 0.18 * jax.random.normal(splits[8], (DT,), jnp.float32), 0.1, 1.9),
        "text_weight": gaussian(splits[9], (DT, 2, HC), DT ** -0.5, 0.09375, ((0, 4), (2, 4))),
        "prompt_length": jax.random.randint(part_splits[10], (1,), TXT // 8, TXT + 1).astype(jnp.int32),
    }


def head_split(values, count):
    return values.reshape(values.shape[0], count, -1).transpose(1, 0, 2)

def reference(video_states, query_self, key_self, value_self, out_weight, cross_gain, query_weight, text_memory, text_gain, text_weight, prompt_length):
    factor = 1.0 / math.sqrt(HD)

    def self_head(operands):
        query_head, key_head, value_head = operands
        scores = jnp.dot(query_head, key_head.T, preferred_element_type=jnp.float32) * factor
        row_top = lax.optimization_barrier(jnp.max(scores, axis=1, keepdims=True))
        weights = jnp.exp(scores - row_top)
        weights_low = weights.astype(jnp.bfloat16)
        return jnp.dot(weights_low, value_head, preferred_element_type=jnp.float32) / lax.optimization_barrier(jnp.sum(weights, axis=1, keepdims=True))
    heads_self = lax.map(self_head, (head_split(query_self, HEADS), head_split(key_self, HEADS), head_split(value_self, HEADS)))
    attn_self = heads_self.transpose(1, 0, 2).reshape(TOKENS, HC).astype(jnp.bfloat16)
    residual_out = (video_states.astype(jnp.float32) + jnp.dot(attn_self, out_weight, preferred_element_type=jnp.float32)).astype(jnp.bfloat16)
    residual_float = residual_out.astype(jnp.float32)
    average = lax.optimization_barrier(jnp.sum(residual_float, axis=1)) / D
    spread = lax.optimization_barrier(jnp.sum(residual_float * residual_float, axis=1)) / D - average * average
    normed = ((residual_float - average[:, None]) * lax.rsqrt(spread[:, None] + 1e-06) * cross_gain).astype(jnp.bfloat16)
    cross_query = jnp.dot(normed, query_weight, preferred_element_type=jnp.float32).astype(jnp.bfloat16)
    memory_float = text_memory.astype(jnp.float32)
    scaled_text = (memory_float * text_gain).astype(jnp.bfloat16)
    text_root = jnp.sqrt(lax.optimization_barrier(jnp.sum(memory_float * memory_float, axis=1)) / DT + 1e-06)
    projected = jnp.dot(scaled_text, text_weight.reshape(DT, 2 * HC), preferred_element_type=jnp.float32)
    text_keyval = (projected / text_root[:, None]).astype(jnp.bfloat16)
    text_keys = text_keyval[:, :HC]
    text_values = text_keyval[:, HC:]
    valid = jnp.arange(TXT, dtype=jnp.int32) < prompt_length[0]

    def cross_head(operands):
        query_head, key_head, value_head = operands
        scores = jnp.dot(query_head, key_head.T, preferred_element_type=jnp.float32) * factor
        scores = jnp.where(valid[None, :], scores, -1e+30)
        weights = jnp.exp(scores)
        weights_low = weights.astype(jnp.bfloat16)
        return jnp.dot(weights_low, value_head, preferred_element_type=jnp.float32) / lax.optimization_barrier(jnp.sum(weights, axis=1, keepdims=True))
    heads_cross = lax.map(cross_head, (head_split(cross_query, HEADS), head_split(text_keys, HEADS), head_split(text_values, HEADS)))
    cross_out = heads_cross.transpose(1, 0, 2).reshape(TOKENS, HC).astype(jnp.bfloat16)
    return (residual_out, cross_out)
```

```python
import functools
import math

import jax
import jax.numpy as jnp
from jax import lax
from jax.experimental import pallas as pl
from jax.experimental.pallas import tpu as pltpu
from jax.sharding import PartitionSpec as P

D = 5120
DT = 4096
HD = 128
FACTOR = 1.0 / math.sqrt(HD)
EXP2 = FACTOR * math.log2(math.e)


def dot(a, b, dims):
    return lax.dot_general(a, b, (dims, ((), ())), preferred_element_type=jnp.float32)


def attend_body(count, first, last, flags, query, *refs):
    blocks = refs[: 2 * count]
    refs = refs[2 * count :]
    if not first:
        stat_in, acc_in = refs[:2]
        refs = refs[2:]
    outs, (stat, acc) = refs[:-2], refs[-2:]
    rows = query.shape[0]
    if not first:
        stat[...] = stat_in[...]
        acc[...] = acc_in[...]
    for n in range(count):
        key, value = blocks[2 * n], blocks[2 * n + 1]

        def fold(key=key, value=value, fresh=first and n == 0):
            scores = dot(key[...], query[...], ((1,), (1,)))
            top = jnp.max(scores, axis=0, keepdims=True)
            if not fresh:
                old = stat[0:1, :]
                top = jnp.maximum(old, top)
            weights = jnp.exp2((scores - top) * EXP2)
            total = jnp.sum(weights, axis=0, keepdims=True)
            mixed = dot(value[...], weights.astype(jnp.bfloat16), ((0,), (0,)))
            if not fresh:
                shrink = jnp.exp2((old - top) * EXP2)
                total = total + stat[1:2, :] * shrink
                mixed = mixed + acc[...] * shrink
            stat[0:1, :] = top
            stat[1:2, :] = total
            acc[...] = mixed

        if first and n == 0:
            fold()
        else:
            pl.when(flags[n] > 0)(fold)
    if last:
        outs[0][...] = (acc[...] / stat[1:2, :]).astype(jnp.bfloat16)
    else:
        outs[0][...] = stat[...]
        outs[1][...] = acc[...]


def attend(flags, query, blocks, state, last):
    rows, width = query.shape
    heads = width // HD
    first = state is None
    count = len(blocks)
    by_head = pl.BlockSpec((rows, HD), lambda h, f: (0, h))
    in_specs = [by_head]
    operands = [query]
    for key, value in blocks:
        spec = pl.BlockSpec((key.shape[0], HD), lambda h, f: (0, h))
        in_specs += [spec, spec]
        operands += [key, value]
    stat_spec = pl.BlockSpec((8, rows), lambda h, f: (h, 0))
    acc_spec = pl.BlockSpec((HD, rows), lambda h, f: (h, 0))
    if not first:
        in_specs += [stat_spec, acc_spec]
        operands += list(state)
    if last:
        out_shape = [jax.ShapeDtypeStruct((width, rows), jnp.bfloat16)]
        out_specs = [acc_spec]
    else:
        out_shape = [
            jax.ShapeDtypeStruct((heads * 8, rows), jnp.float32),
            jax.ShapeDtypeStruct((width, rows), jnp.float32),
        ]
        out_specs = [stat_spec, acc_spec]
    return pl.pallas_call(
        functools.partial(attend_body, count, first, last),
        out_shape=out_shape,
        grid_spec=pltpu.PrefetchScalarGridSpec(
            num_scalar_prefetch=1,
            grid=(heads,),
            in_specs=in_specs,
            out_specs=out_specs,
            scratch_shapes=[pltpu.VMEM((8, rows), jnp.float32), pltpu.VMEM((HD, rows), jnp.float32)],
        ),
        name="attend",
    )(flags, *operands)


def project_body(order, mixed, weight, out):
    out[...] = dot(mixed[...], weight[...], ((0,), (0,))).astype(jnp.bfloat16)


def project(order, mixed, chunk, chunks, weight, pieces):
    width, rows = mixed.shape
    rows = rows // chunks
    piece = weight.shape[1] // pieces
    count = order.shape[0]
    return pl.pallas_call(
        project_body,
        out_shape=jax.ShapeDtypeStruct((rows, piece * count), jnp.bfloat16),
        grid_spec=pltpu.PrefetchScalarGridSpec(
            num_scalar_prefetch=1,
            grid=(count,),
            in_specs=[
                pl.BlockSpec((width, rows), lambda p, o: (0, chunk)),
                pl.BlockSpec((width, piece), lambda p, o: (0, o[p])),
            ],
            out_specs=pl.BlockSpec((rows, piece), lambda p, o: (0, p)),
        ),
        name="project",
    )(order, mixed, weight)


def cross_body(heads, slots, order, tokens, *refs):
    pieces = order.shape[0]
    parts = refs[:pieces]
    gain, weight, text, out, average, scale, acc = refs[pieces:]
    step = pl.program_id(0)

    @pl.when(step == 0)
    def _():
        total = 0.0
        squares = 0.0
        for part in parts:
            value = part[...].astype(jnp.float32)
            total = total + jnp.sum(value, axis=1, keepdims=True)
            squares = squares + jnp.sum(value * value, axis=1, keepdims=True)
        mean = total / D
        average[...] = mean
        scale[...] = lax.rsqrt(squares / D - mean * mean + 1e-06)
        acc[...] = jnp.zeros_like(acc)

    for n, part in enumerate(parts):

        @pl.when(step == n)
        def _(part=part):
            value = part[...].astype(jnp.float32)
            normed = ((value - average[...]) * scale[...] * gain[...]).astype(jnp.bfloat16)
            acc[...] += dot(normed, weight[...], ((1,), (0,)))

    @pl.when(step == pieces - 1)
    def _():
        width = heads * HD
        query = acc[...].astype(jnp.bfloat16)
        share = text.shape[0] // slots
        token = lax.broadcasted_iota(jnp.int32, (1, slots * share), 1)
        shift = jnp.zeros_like(token)
        for n in range(slots):
            shift = jnp.where(token >= n * share, (tokens[n] - n) * share, shift)
        valid = token + shift < tokens[slots]
        for h in range(heads):
            keys = text[:, h * HD : (h + 1) * HD]
            values = text[:, width + h * HD : width + (h + 1) * HD]
            scores = dot(query[:, h * HD : (h + 1) * HD], keys, ((1,), (1,))) * FACTOR
            weights = jnp.exp(jnp.where(valid, scores, -1e30))
            mixed = dot(weights.astype(jnp.bfloat16), values, ((1,), (0,)))
            out[:, h * HD : (h + 1) * HD] = (
                mixed / jnp.sum(weights, axis=1, keepdims=True)
            ).astype(jnp.bfloat16)


def cross(order, tokens, parts, gain, weight, text, heads, slots):
    pieces = len(parts)
    rows, piece = parts[0].shape
    width = weight.shape[1]
    whole = lambda shape: pl.BlockSpec(shape, lambda p, o, t: (0,) * len(shape))
    return pl.pallas_call(
        functools.partial(cross_body, heads, slots),
        out_shape=jax.ShapeDtypeStruct((rows, width), jnp.bfloat16),
        grid_spec=pltpu.PrefetchScalarGridSpec(
            num_scalar_prefetch=2,
            grid=(pieces,),
            in_specs=[whole((rows, piece))] * pieces
            + [
                pl.BlockSpec((1, piece), lambda p, o, t: (0, p)),
                pl.BlockSpec((piece, width), lambda p, o, t: (o[p], 0)),
                whole(text.shape),
            ],
            out_specs=whole((rows, width)),
            scratch_shapes=[
                pltpu.VMEM((rows, 1), jnp.float32),
                pltpu.VMEM((rows, 1), jnp.float32),
                pltpu.VMEM((rows, width), jnp.float32),
            ],
        ),
        name="cross",
    )(order, tokens, *parts, gain, weight, text)


def shards(
    seq_size,
    tensor_size,
    video_states,
    query_self,
    key_self,
    value_self,
    out_weight,
    cross_gain,
    query_weight,
    text_memory,
    text_gain,
    text_weight,
    prompt_length,
):
    local_rows, local_width = query_self.shape
    heads = local_width // HD
    place = lax.axis_index("seq")
    slot = lax.axis_index("tensor")
    paired = tensor_size == 4

    def right(x, most=seq_size):
        return lax.ppermute(x, "seq", [(n, n + 1) for n in range(min(most, seq_size - 1))])

    def left(x, most=seq_size):
        last = seq_size - 1
        return lax.ppermute(x, "seq", [(last - n, last - n - 1) for n in range(min(most, last))])

    def swap(x, bit):
        return lax.ppermute(x, "tensor", [(n, n ^ bit) for n in range(tensor_size)])

    from_left = from_right = (key_self, value_self)
    state = attend(jnp.ones((1,), jnp.int32), query_self, [(key_self, value_self)], None, seq_size == 1)
    for step in range(1, seq_size):
        from_left = tuple(right(x) for x in from_left)
        from_right = tuple(left(x) for x in from_right)
        flags = jnp.stack([place >= step, place + step < seq_size]).astype(jnp.int32)
        state = attend(flags, query_self, [from_left, from_right], state, step == seq_size - 1)
    mixed = state[0]

    memory_float = text_memory.astype(jnp.float32)
    scaled_text = (memory_float * text_gain).astype(jnp.bfloat16)
    square_part = jnp.sum(memory_float * memory_float, axis=1)
    text_part = jnp.dot(
        scaled_text,
        text_weight.reshape(text_weight.shape[0], -1),
        preferred_element_type=jnp.float32,
    )
    share = text_part.shape[0] // seq_size

    def rows_of(array, owner):
        return lax.dynamic_slice_in_dim(array, jnp.clip(owner, 0, seq_size - 1) * share, share)

    rightward = leftward = None
    for step in range(1, seq_size):
        to_right = rows_of(text_part, seq_size - step + place), rows_of(square_part, seq_size - step + place)
        to_left = rows_of(text_part, place - seq_size + step), rows_of(square_part, place - seq_size + step)
        if step > 1:
            to_right = tuple(a + b.astype(jnp.float32) for a, b in zip(to_right, rightward))
            to_left = tuple(a + b.astype(jnp.float32) for a, b in zip(to_left, leftward))
        rightward = right(to_right[0].astype(jnp.bfloat16), step), right(to_right[1], step)
        leftward = left(to_left[0].astype(jnp.bfloat16), step), left(to_left[1], step)
    text_sum, square_sum = (
        rows_of(own, place) + a.astype(jnp.float32) + b.astype(jnp.float32)
        for own, a, b in zip((text_part, square_part), rightward, leftward)
    )
    text_low = (text_sum / jnp.sqrt(square_sum / DT + 1e-06)[:, None]).astype(jnp.bfloat16)
    lefts, rights = [text_low], [text_low]
    for step in range(1, seq_size):
        lefts.append(right(lefts[-1]))
        rights.append(left(rights[-1]))
    text_all = jnp.concatenate(
        [text_low] + [jnp.where(place >= n, lefts[n], rights[seq_size - n]) for n in range(1, seq_size)]
    )
    tokens = jnp.concatenate(
        [(place - jnp.arange(seq_size)) % seq_size, prompt_length]
    ).astype(jnp.int32)

    chunks = 3 if local_rows % (3 * 128) == 0 else 1
    chunk_rows = local_rows // chunks
    outs, residuals = [], []
    if paired:
        theirs = jnp.stack([slot ^ 1, slot ^ 3]).astype(jnp.int32)
        mine = jnp.stack([slot, slot ^ 2]).astype(jnp.int32)
        order = jnp.stack([slot, slot ^ 2, slot ^ 1, slot ^ 3]).astype(jnp.int32)
        gain_two = jnp.stack([cross_gain, swap(cross_gain, 2)])
        gain_all = jnp.concatenate([gain_two, swap(gain_two, 1)]).reshape(1, -1)
    else:
        order = jnp.arange(tensor_size, dtype=jnp.int32)
        gain_all = lax.all_gather(cross_gain, "tensor", axis=0, tiled=True).reshape(1, -1)
    piece = cross_gain.shape[0]
    for n in range(chunks):
        video = video_states[n * chunk_rows : (n + 1) * chunk_rows].astype(jnp.float32)
        if paired:
            sent = swap(project(theirs, mixed, n, chunks, out_weight, tensor_size), 1)
            kept = project(mine, mixed, n, chunks, out_weight, tensor_size)
            over = (kept[:, piece:].astype(jnp.float32) + sent[:, piece:].astype(jnp.float32)).astype(jnp.bfloat16)
            other = swap(over, 2)
            residual = (
                video
                + kept[:, :piece].astype(jnp.float32)
                + sent[:, :piece].astype(jnp.float32)
                + other.astype(jnp.float32)
            ).astype(jnp.bfloat16)
            across = swap(residual, 2)
            parts = [residual, across, swap(residual, 1), swap(across, 1)]
        else:
            partial = project(order, mixed, n, chunks, out_weight, tensor_size)
            summed = lax.psum_scatter(partial, "tensor", scatter_dimension=1, tiled=True)
            residual = (video + summed.astype(jnp.float32)).astype(jnp.bfloat16)
            gathered = lax.all_gather(residual, "tensor", axis=1, tiled=True)
            parts = [gathered[:, m * piece : (m + 1) * piece] for m in range(tensor_size)]
        residuals.append(residual)
        outs.append(cross(order, tokens, parts, gain_all, query_weight, text_all, heads, seq_size))
    return (jnp.concatenate(residuals), jnp.concatenate(outs))


def solution(mesh):
    in_specs = (
        P(("groups", "seq"), "tensor"),
        P(("groups", "seq"), "tensor"),
        P(("groups", "seq"), "tensor"),
        P(("groups", "seq"), "tensor"),
        P("tensor", None),
        P("tensor"),
        P(None, "tensor"),
        P("groups", "seq"),
        P("seq"),
        P("seq", None, "tensor"),
        P("groups"),
    )
    out_specs = (P(("groups", "seq"), "tensor"), P(("groups", "seq"), "tensor"))
    body = functools.partial(shards, mesh.shape["seq"], mesh.shape["tensor"])
    return jax.shard_map(body, mesh=mesh, in_specs=in_specs, out_specs=out_specs, check_vma=False)
```

```python
import functools
import math

import jax
import jax.numpy as jnp
from jax import lax
from jax.experimental import pallas as pl
from jax.experimental.pallas import tpu as pltpu
from jax.sharding import PartitionSpec as P

D = 5120
DT = 4096
HD = 128
FACTOR = 1.0 / math.sqrt(HD)
EXP2 = FACTOR * math.log2(math.e)

ATTEND_VMEM = 16 << 20
PROJECT_VMEM = 24 << 20
CROSS_VMEM = 28 << 20


def dot(a, b, dims):
    return lax.dot_general(a, b, (dims, ((), ())), preferred_element_type=jnp.float32)


def attend_body(per, checks, first, last, info, query, *refs):
    count = len(checks)
    blocks = refs[: 2 * count]
    refs = refs[2 * count :]
    if not first:
        stat_in, acc_in = refs[:2]
        refs = refs[2:]
    outs, (stat, acc) = refs[:-2], refs[-2:]
    if not first:
        stat[...] = stat_in[...]
        acc[...] = acc_in[...]
    for n, check in enumerate(checks):
        key, value = blocks[2 * n], blocks[2 * n + 1]
        fresh = first and n == 0

        def fold(key=key, value=value, fresh=fresh):
            for h in range(per):
                cols = slice(h * HD, (h + 1) * HD)
                top_row, sum_row = slice(8 * h, 8 * h + 1), slice(8 * h + 1, 8 * h + 2)
                scores = dot(key[:, cols], query[:, cols], ((1,), (1,)))
                top = jnp.max(scores, axis=0, keepdims=True)
                if not fresh:
                    old = stat[top_row, :]
                    top = jnp.maximum(old, top)
                weights = jnp.exp2((scores - top) * EXP2)
                total = jnp.sum(weights, axis=0, keepdims=True)
                mixed = dot(value[:, cols], weights.astype(jnp.bfloat16), ((0,), (0,)))
                if not fresh:
                    shrink = jnp.exp2((old - top) * EXP2)
                    total = total + stat[sum_row, :] * shrink
                    mixed = mixed + acc[cols, :] * shrink
                stat[top_row, :] = top
                stat[sum_row, :] = total
                acc[cols, :] = mixed

        if check is None:
            fold()
        else:
            pl.when(info[check] > 0)(fold)
    if last:
        for h in range(per):
            cols = slice(h * HD, (h + 1) * HD)
            outs[0][cols, :] = (acc[cols, :] / stat[8 * h + 1 : 8 * h + 2, :]).astype(jnp.bfloat16)
    else:
        outs[0][...] = stat[...]
        outs[1][...] = acc[...]


def attend(info, query, blocks, state, last, per, groups):
    rows = query[0].shape[0]
    first = state is None

    def spec(pair):
        array, index = pair
        return pl.BlockSpec((array.shape[0], per * HD), lambda g, i: (0, index(g)))

    in_specs = [spec(query)]
    operands = [query[0]]
    for key, value, check in blocks:
        in_specs += [spec(key), spec(value)]
        operands += [key[0], value[0]]
    stat_spec = pl.BlockSpec((8 * per, rows), lambda g, i: (g, 0))
    acc_spec = pl.BlockSpec((HD * per, rows), lambda g, i: (g, 0))
    if not first:
        in_specs += [stat_spec, acc_spec]
        operands += list(state)
    width = HD * per * groups
    if last:
        out_shape = [jax.ShapeDtypeStruct((width, rows), jnp.bfloat16)]
        out_specs = [acc_spec]
    else:
        out_shape = [
            jax.ShapeDtypeStruct((8 * per * groups, rows), jnp.float32),
            jax.ShapeDtypeStruct((width, rows), jnp.float32),
        ]
        out_specs = [stat_spec, acc_spec]
    return pl.pallas_call(
        functools.partial(attend_body, per, [b[2] for b in blocks], first, last),
        out_shape=out_shape,
        grid_spec=pltpu.PrefetchScalarGridSpec(
            num_scalar_prefetch=1,
            grid=(groups,),
            in_specs=in_specs,
            out_specs=out_specs,
            scratch_shapes=[
                pltpu.VMEM((8 * per, rows), jnp.float32),
                pltpu.VMEM((HD * per, rows), jnp.float32),
            ],
        ),
        compiler_params=pltpu.CompilerParams(vmem_limit_bytes=ATTEND_VMEM),
        name="attend",
    )(info, *operands)


def project_body(check, chunks, info, *refs):
    mixed, weight, outs = refs[:-chunks - 1], refs[-chunks - 1], refs[-chunks:]
    if check is None:
        total = dot(mixed[0][...], weight[...], ((0,), (0,)))
    else:
        near, far, rest = mixed
        lead = jnp.where(info[check] > 0, far[...], near[...])
        cut = lead.shape[0]
        total = dot(lead, weight[:cut, :], ((0,), (0,))) + dot(rest[...], weight[cut:, :], ((0,), (0,)))
    rows = total.shape[0] // chunks
    for n, out in enumerate(outs):
        out[...] = total[n * rows : (n + 1) * rows].astype(jnp.bfloat16)


def project(info, mixed, check, chunks, weight, pieces, base, count):
    rows = mixed[0].shape[1]
    piece = weight.shape[1] // pieces
    return pl.pallas_call(
        functools.partial(project_body, check, chunks),
        out_shape=[jax.ShapeDtypeStruct((rows // chunks, piece * count), jnp.bfloat16)] * chunks,
        grid_spec=pltpu.PrefetchScalarGridSpec(
            num_scalar_prefetch=1,
            grid=(count,),
            in_specs=[pl.BlockSpec(m.shape, lambda p, i: (0, 0)) for m in mixed]
            + [pl.BlockSpec((weight.shape[0], piece), lambda p, i: (0, i[base + p]))],
            out_specs=[pl.BlockSpec((rows // chunks, piece), lambda p, i: (0, p))] * chunks,
        ),
        compiler_params=pltpu.CompilerParams(vmem_limit_bytes=PROJECT_VMEM),
        name="project",
    )(info, *mixed, weight)


def cross_body(heads, base, limit, info, *refs):
    pieces = 4 if base is None else base[1]
    parts = refs[:pieces]
    gain, weight = refs[pieces : pieces + 2]
    texts = refs[pieces + 2 : -4]
    out, average, scale, acc = refs[-4:]
    step = pl.program_id(0)

    @pl.when(step == 0)
    def _():
        total = 0.0
        squares = 0.0
        for part in parts:
            value = part[...].astype(jnp.float32)
            total = total + jnp.sum(value, axis=1, keepdims=True)
            squares = squares + jnp.sum(value * value, axis=1, keepdims=True)
        mean = total / D
        average[...] = mean
        scale[...] = lax.rsqrt(squares / D - mean * mean + 1e-06)
        acc[...] = jnp.zeros_like(acc)

    for n, part in enumerate(parts):

        @pl.when(step == n)
        def _(part=part):
            value = part[...].astype(jnp.float32)
            normed = ((value - average[...]) * scale[...] * gain[...]).astype(jnp.bfloat16)
            acc[...] += dot(normed, weight[...], ((1,), (0,)))

    @pl.when(step == pieces - 1)
    def _():
        width = heads * HD
        query = acc[...].astype(jnp.bfloat16)
        for h in range(heads):
            cols = slice(h * HD, (h + 1) * HD)
            total = 0.0
            mixed = 0.0
            start = 0
            for text in texts:
                token = start + lax.broadcasted_iota(jnp.int32, (1, text.shape[0]), 1)
                start += text.shape[0]
                scores = dot(query[:, cols], text[:, cols], ((1,), (1,))) * FACTOR
                weights = jnp.exp(jnp.where(token < info[limit], scores, -1e30))
                total = total + jnp.sum(weights, axis=1, keepdims=True)
                values = text[:, width + h * HD : width + (h + 1) * HD]
                mixed = mixed + dot(weights.astype(jnp.bfloat16), values, ((1,), (0,)))
            out[:, cols] = (mixed / total).astype(jnp.bfloat16)


def cross(info, base, limit, parts, gain, weight, texts, heads):
    pieces = len(parts)
    rows, piece = parts[0].shape
    width = weight.shape[1]
    whole = lambda shape: pl.BlockSpec(shape, lambda p, i: (0,) * len(shape))
    return pl.pallas_call(
        functools.partial(cross_body, heads, (base, pieces), limit),
        out_shape=jax.ShapeDtypeStruct((rows, width), jnp.bfloat16),
        grid_spec=pltpu.PrefetchScalarGridSpec(
            num_scalar_prefetch=1,
            grid=(pieces,),
            in_specs=[whole((rows, piece))] * pieces
            + [
                pl.BlockSpec((1, piece), lambda p, i: (0, p)),
                pl.BlockSpec((piece, width), lambda p, i: (i[base + p], 0)),
            ]
            + [whole(text.shape) for text in texts],
            out_specs=whole((rows, width)),
            scratch_shapes=[
                pltpu.VMEM((rows, 1), jnp.float32),
                pltpu.VMEM((rows, 1), jnp.float32),
                pltpu.VMEM((rows, width), jnp.float32),
            ],
        ),
        compiler_params=pltpu.CompilerParams(vmem_limit_bytes=CROSS_VMEM),
        name="cross",
    )(info, *parts, gain, weight, *texts)


def self_line(info, left_check, query, key, value, heads, seq_size, right, left):
    same = lambda g: g
    pair = lambda k, v, check: ((k, same), (v, same), check)
    from_left = from_right = (key, value)
    state = attend(info, (query, same), [pair(key, value, None)], None, seq_size == 1, 1, heads)
    for step in range(1, seq_size):
        from_left = tuple(right(x) for x in from_left)
        from_right = tuple(left(x) for x in from_right)
        blocks = [
            pair(*from_left, left_check + 2 * (step - 1)),
            pair(*from_right, left_check + 2 * (step - 1) + 1),
        ]
        state = attend(info, (query, same), blocks, state, step == seq_size - 1, 1, heads)
    return state[0]


def text_line(text_part, square_part, place, seq_size, right, left):
    share = text_part.shape[0] // seq_size

    def rows_of(array, owner):
        return lax.dynamic_slice_in_dim(array, jnp.clip(owner, 0, seq_size - 1) * share, share)

    rightward = leftward = None
    for step in range(1, seq_size):
        ahead, behind = place + seq_size - step, place - seq_size + step
        to_right = rows_of(text_part, ahead), rows_of(square_part, ahead)
        to_left = rows_of(text_part, behind), rows_of(square_part, behind)
        if step > 1:
            to_right = tuple(a + b.astype(jnp.float32) for a, b in zip(to_right, rightward))
            to_left = tuple(a + b.astype(jnp.float32) for a, b in zip(to_left, leftward))
        rightward = right(to_right[0].astype(jnp.bfloat16), step), right(to_right[1], step)
        leftward = left(to_left[0].astype(jnp.bfloat16), step), left(to_left[1], step)
    text_sum, square_sum = (
        rows_of(own, place) + a.astype(jnp.float32) + b.astype(jnp.float32)
        for own, a, b in zip((text_part, square_part), rightward, leftward)
    )
    text_low = (text_sum / jnp.sqrt(square_sum / DT + 1e-06)[:, None]).astype(jnp.bfloat16)
    return lax.all_gather(text_low, "seq", axis=0, tiled=True)


def shards(
    seq_size,
    tensor_size,
    video_states,
    query_self,
    key_self,
    value_self,
    out_weight,
    cross_gain,
    query_weight,
    text_memory,
    text_gain,
    text_weight,
    prompt_length,
):
    local_rows, local_width = query_self.shape
    heads = local_width // HD
    place = lax.axis_index("seq")
    slot = lax.axis_index("tensor")
    paired = tensor_size == 4
    four = seq_size == 4 and heads == 6 and text_memory.shape[0] * 3 == local_rows * 4
    piece = cross_gain.shape[0]

    def right(x, most=seq_size):
        return lax.ppermute(x, "seq", [(n, n + 1) for n in range(min(most, seq_size - 1))])

    def left(x, most=seq_size):
        last = seq_size - 1
        return lax.ppermute(x, "seq", [(last - n, last - n - 1) for n in range(min(most, last))])

    def swap(x, bit):
        return lax.ppermute(x, "tensor", [(n, n ^ bit) for n in range(tensor_size)])

    is_end = (place == 0) | (place == seq_size - 1)
    if paired:
        order = [slot ^ 1, slot ^ 3, slot, slot ^ 2, slot ^ 1, slot ^ 3]
    else:
        order = [jnp.int32(n) for n in range(tensor_size)]
    scalars = [prompt_length[0], is_end, ~is_end] + order
    line_check = len(scalars)
    for step in range(1, seq_size):
        scalars += [place >= step, place + step < seq_size]
    info = jnp.stack([s.astype(jnp.int32) for s in scalars])
    LIMIT, END, MIDDLE, ORDER = 0, 1, 2, 3

    def text_parts(memory, gain, weight):
        memory_float = memory.astype(jnp.float32)
        scaled_text = (memory_float * gain).astype(jnp.bfloat16)
        square_part = jnp.sum(memory_float * memory_float, axis=1)
        text_part = jnp.dot(
            scaled_text, weight.reshape(weight.shape[0], -1), preferred_element_type=jnp.float32
        )
        return text_part, square_part

    chunks = 2 if local_rows % 32 == 0 else 1
    if four:
        outer = lambda x: lax.ppermute(x, "seq", [(0, 1), (1, 0), (2, 3), (3, 2)])
        inner = lambda x: lax.ppermute(x, "seq", [(0, 0), (1, 2), (2, 1), (3, 3)])
        lent = 2
        cut = lent * HD
        kept_pack = jnp.concatenate([key_self[:, cut:], value_self[:, cut:]], axis=1)
        lent_pack = jnp.concatenate(
            [key_self[:, :cut], value_self[:, :cut], query_self[:, :cut], query_self[:, :cut]], axis=1
        )
        kept = lambda x, check: ((x, lambda g: g), (x, lambda g: g + 2), check)
        lend = lambda x, check: ((x, lambda g: 0), (x, lambda g: 1), check)
        query_kept = (query_self, lambda g: g + 1)
        outer_1, inner_1 = outer(kept_pack), inner(kept_pack)
        state = attend(info, query_kept, [kept(kept_pack, None)], None, False, 2, 2)
        (text_memory, text_gain, text_weight, cross_gain), state = lax.optimization_barrier(
            ((text_memory, text_gain, text_weight, cross_gain), state)
        )
        text_part, square_part = text_parts(text_memory, text_gain, text_weight)
        text_low = text_part.astype(jnp.bfloat16)
        square_sum = square_part + outer(square_part)
        root = jnp.sqrt((square_sum + inner(square_sum)) / DT + 1e-06)
        low = place < seq_size // 2
        half = text_part.shape[0] // 2
        share = half // 2
        third = local_width * 2 // 3

        def pack(x):
            rows = [
                jnp.concatenate([x[:share, n * third : (n + 1) * third], x[share:, n * third : (n + 1) * third]], axis=1)
                for n in range(3)
            ]
            return jnp.concatenate(rows)

        def unpack(x):
            cols = [
                jnp.concatenate([x[n * share : (n + 1) * share, :third], x[n * share : (n + 1) * share, third:]])
                for n in range(3)
            ]
            return jnp.concatenate(cols, axis=1)

        outer_2, inner_2 = outer(jnp.where(is_end, lent_pack, inner_1)), inner(outer_1)
        state = attend(info, query_kept, [kept(outer_1, None), kept(inner_1, MIDDLE)], state, False, 2, 2)
        outer_3 = outer(jnp.where(is_end, pack(text_low[:half]), inner_2))
        inner_3, inner_4 = inner(lent_pack[:, : 2 * cut]), inner(outer_2[:, : 2 * cut])
        state = attend(info, query_kept, [kept(outer_2, END), kept(inner_2, MIDDLE)], state, False, 2, 2)
        query_lent = (jnp.concatenate([lent_pack[:, 2 * cut : 3 * cut], outer_2[:, 2 * cut : 3 * cut]], axis=1), lambda g: g)
        loan = attend(info, query_lent, [lend(lent_pack, None), lend(outer_2, MIDDLE)], None, False, 2, 2)
        loan = attend(info, query_lent, [lend(inner_3, MIDDLE)], loan, False, 2, 2)
        loan = attend(info, query_lent, [lend(inner_4, MIDDLE)], loan, True, 2, 2)[0]
        back = outer(loan[cut:])
        rest = attend(info, query_kept, [kept(outer_3, END)], state, True, 2, 2)[0]
        mixed = [loan[:cut], back, rest]
        mixed_check = END

        late, outer_3 = lax.optimization_barrier((text_low[half:], outer_3))
        arrived = [unpack(outer_3), outer(late)]
        texts = []
        for n in range(2):
            rows = slice(n * half, (n + 1) * half)
            pair_sum = text_part[rows] + arrived[n].astype(jnp.float32)
            first, second = pair_sum[:share], pair_sum[share:]
            given = inner(jnp.where(low, second, first).astype(jnp.bfloat16))
            own_root = jnp.where(low, root[rows][:share], root[rows][share:])
            own = ((jnp.where(low, first, second) + given.astype(jnp.float32)) / own_root[:, None]).astype(jnp.bfloat16)
            other = inner(own)
            both = jnp.concatenate([jnp.where(low, own, other), jnp.where(low, other, own)])
            texts.append(jnp.where(is_end, outer(both), both))
    else:
        mixed = [self_line(info, line_check, query_self, key_self, value_self, heads, seq_size, right, left)]
        mixed_check = None
        text_part, square_part = text_parts(text_memory, text_gain, text_weight)
        texts = [text_line(text_part, square_part, place, seq_size, right, left)]

    if paired:
        gain_two = jnp.stack([cross_gain, swap(cross_gain, 2)])
        gain_all = jnp.concatenate([gain_two, swap(gain_two, 1)]).reshape(1, -1)
        theirs = project(info, mixed, mixed_check, chunks, out_weight, tensor_size, ORDER, 2)
        mine = project(info, mixed, mixed_check, chunks, out_weight, tensor_size, ORDER + 2, 2)
        sents = [swap(x, 1) for x in theirs]
    else:
        gain_all = lax.all_gather(cross_gain, "tensor", axis=0, tiled=True).reshape(1, -1)
        partials = project(info, mixed, mixed_check, chunks, out_weight, tensor_size, ORDER, tensor_size)
    chunk_rows = local_rows // chunks
    outs, residuals = [], []
    for n in range(chunks):
        video = video_states[n * chunk_rows : (n + 1) * chunk_rows].astype(jnp.float32)
        if paired:
            sent, own = sents[n].astype(jnp.float32), mine[n].astype(jnp.float32)
            other = swap((own[:, piece:] + sent[:, piece:]).astype(jnp.bfloat16), 2)
            residual = (video + own[:, :piece] + sent[:, :piece] + other.astype(jnp.float32)).astype(jnp.bfloat16)
            across = swap(residual, 2)
            parts = [residual, across, swap(residual, 1), swap(across, 1)]
            base = ORDER + 2
        else:
            summed = lax.psum_scatter(partials[n], "tensor", scatter_dimension=1, tiled=True)
            residual = (video + summed.astype(jnp.float32)).astype(jnp.bfloat16)
            gathered = lax.all_gather(residual, "tensor", axis=1, tiled=True)
            parts = [gathered[:, m * piece : (m + 1) * piece] for m in range(tensor_size)]
            base = ORDER
        residuals.append(residual)
        outs.append(cross(info, base, LIMIT, parts, gain_all, query_weight, texts, heads))
    return (jnp.concatenate(residuals), jnp.concatenate(outs))


def solution(mesh):
    in_specs = (
        P(("groups", "seq"), "tensor"),
        P(("groups", "seq"), "tensor"),
        P(("groups", "seq"), "tensor"),
        P(("groups", "seq"), "tensor"),
        P("tensor", None),
        P("tensor"),
        P(None, "tensor"),
        P("groups", "seq"),
        P("seq"),
        P("seq", None, "tensor"),
        P("groups"),
    )
    out_specs = (P(("groups", "seq"), "tensor"), P(("groups", "seq"), "tensor"))
    body = functools.partial(shards, mesh.shape["seq"], mesh.shape["tensor"])
    return jax.shard_map(body, mesh=mesh, in_specs=in_specs, out_specs=out_specs, check_vma=False)
```

```python
import functools
import math

import jax
import jax.numpy as jnp
from jax import lax
from jax.experimental import pallas as pl
from jax.experimental.pallas import tpu as pltpu
from jax.sharding import PartitionSpec as P


D = 5120
DT = 4096
HD = 128
FACTOR = 1.0 / math.sqrt(HD)
EXP2 = FACTOR * math.log2(math.e)

ATTEND_VMEM = 16 << 20
PROJECT_VMEM = 24 << 20
CROSS_VMEM = 28 << 20


def dot(a, b, dims):
    return lax.dot_general(a, b, (dims, ((), ())), preferred_element_type=jnp.float32)


def attend_body(per, checks, first, last, info, query, *refs):
    count = len(checks)
    blocks = refs[: 2 * count]
    refs = refs[2 * count :]
    if not first:
        stat_in, acc_in = refs[:2]
        refs = refs[2:]
    outs, (stat, acc) = refs[:-2], refs[-2:]
    if not first:
        stat[...] = stat_in[...]
        acc[...] = acc_in[...]
    for n, check in enumerate(checks):
        key, value = blocks[2 * n], blocks[2 * n + 1]
        fresh = first and n == 0

        def fold(key=key, value=value, fresh=fresh):
            for h in range(per):
                cols = slice(h * HD, (h + 1) * HD)
                top_row, sum_row = slice(8 * h, 8 * h + 1), slice(8 * h + 1, 8 * h + 2)
                scores = dot(key[:, cols], query[:, cols], ((1,), (1,)))
                top = jnp.max(scores, axis=0, keepdims=True)
                if not fresh:
                    old = stat[top_row, :]
                    top = jnp.maximum(old, top)
                weights = jnp.exp2((scores - top) * EXP2)
                total = jnp.sum(weights, axis=0, keepdims=True)
                mixed = dot(value[:, cols], weights.astype(jnp.bfloat16), ((0,), (0,)))
                if not fresh:
                    shrink = jnp.exp2((old - top) * EXP2)
                    total = total + stat[sum_row, :] * shrink
                    mixed = mixed + acc[cols, :] * shrink
                stat[top_row, :] = top
                stat[sum_row, :] = total
                acc[cols, :] = mixed

        if check is None:
            fold()
        else:
            pl.when(info[check] > 0)(fold)
    if last:
        for h in range(per):
            cols = slice(h * HD, (h + 1) * HD)
            outs[0][cols, :] = (acc[cols, :] / stat[8 * h + 1 : 8 * h + 2, :]).astype(jnp.bfloat16)
    else:
        outs[0][...] = stat[...]
        outs[1][...] = acc[...]


def attend(info, query, blocks, state, last, per, groups):
    rows = query[0].shape[0]
    first = state is None

    def spec(pair):
        array, index = pair
        return pl.BlockSpec((array.shape[0], per * HD), lambda g, i: (0, index(g)))

    in_specs = [spec(query)]
    operands = [query[0]]
    for key, value, check in blocks:
        in_specs += [spec(key), spec(value)]
        operands += [key[0], value[0]]
    stat_spec = pl.BlockSpec((8 * per, rows), lambda g, i: (g, 0))
    acc_spec = pl.BlockSpec((HD * per, rows), lambda g, i: (g, 0))
    if not first:
        in_specs += [stat_spec, acc_spec]
        operands += list(state)
    width = HD * per * groups
    if last:
        out_shape = [jax.ShapeDtypeStruct((width, rows), jnp.bfloat16)]
        out_specs = [acc_spec]
    else:
        out_shape = [
            jax.ShapeDtypeStruct((8 * per * groups, rows), jnp.float32),
            jax.ShapeDtypeStruct((width, rows), jnp.float32),
        ]
        out_specs = [stat_spec, acc_spec]
    return pl.pallas_call(
        functools.partial(attend_body, per, [b[2] for b in blocks], first, last),
        out_shape=out_shape,
        grid_spec=pltpu.PrefetchScalarGridSpec(
            num_scalar_prefetch=1,
            grid=(groups,),
            in_specs=in_specs,
            out_specs=out_specs,
            scratch_shapes=[
                pltpu.VMEM((8 * per, rows), jnp.float32),
                pltpu.VMEM((HD * per, rows), jnp.float32),
            ],
        ),
        compiler_params=pltpu.CompilerParams(vmem_limit_bytes=ATTEND_VMEM),
        name="attend",
    )(info, *operands)


def project_body(check, info, *refs):
    mixed, weight, out = refs[:-2], refs[-2], refs[-1]
    if check is None:
        total = dot(mixed[0][...], weight[...], ((0,), (0,)))
    else:
        near, far, rest = mixed
        lead = jnp.where(info[check] > 0, far[...], near[...])
        cut = lead.shape[0]
        total = dot(lead, weight[:cut, :], ((0,), (0,))) + dot(rest[...], weight[cut:, :], ((0,), (0,)))
    out[...] = total.astype(jnp.bfloat16)


def project(info, mixed, check, start, rows, weight, pieces, base, count):
    piece = weight.shape[1] // pieces
    return pl.pallas_call(
        functools.partial(project_body, check),
        out_shape=jax.ShapeDtypeStruct((rows, piece * count), jnp.bfloat16),
        grid_spec=pltpu.PrefetchScalarGridSpec(
            num_scalar_prefetch=1,
            grid=(count,),
            in_specs=[pl.BlockSpec((m.shape[0], rows), lambda p, i: (0, start // rows)) for m in mixed]
            + [pl.BlockSpec((weight.shape[0], piece), lambda p, i: (0, i[base + p]))],
            out_specs=pl.BlockSpec((rows, piece), lambda p, i: (0, p)),
        ),
        compiler_params=pltpu.CompilerParams(vmem_limit_bytes=PROJECT_VMEM),
        name="project",
    )(info, *mixed, weight)


def cross_body(heads, pieces, count, limit, info, *refs):
    parts = refs[:pieces]
    gain, weight = refs[pieces : pieces + 2]
    texts = refs[pieces + 2 : pieces + 2 + count]
    out, average, scale, acc = refs[-4:]
    step = pl.program_id(0)

    @pl.when(step == 0)
    def _():
        total = 0.0
        squares = 0.0
        for part in parts:
            value = part[...].astype(jnp.float32)
            total = total + jnp.sum(value, axis=1, keepdims=True)
            squares = squares + jnp.sum(value * value, axis=1, keepdims=True)
        mean = total / D
        average[...] = mean
        scale[...] = lax.rsqrt(squares / D - mean * mean + 1e-06)
        acc[...] = jnp.zeros_like(acc)

    for n, part in enumerate(parts):

        @pl.when(step == n)
        def _(part=part):
            value = part[...].astype(jnp.float32)
            normed = ((value - average[...]) * scale[...] * gain[...]).astype(jnp.bfloat16)
            acc[...] += dot(normed, weight[...], ((1,), (0,)))

    @pl.when(step == pieces - 1)
    def _():
        width = heads * HD
        query = acc[...].astype(jnp.bfloat16)
        for h in range(heads):
            cols = slice(h * HD, (h + 1) * HD)
            total = 0.0
            mixed = 0.0
            start = 0
            for text in texts:
                token = start + lax.broadcasted_iota(jnp.int32, (1, text.shape[0]), 1)
                start += text.shape[0]
                scores = dot(query[:, cols], text[:, cols], ((1,), (1,))) * FACTOR
                weights = jnp.exp(jnp.where(token < info[limit], scores, -1e30))
                total = total + jnp.sum(weights, axis=1, keepdims=True)
                values = text[:, width + h * HD : width + (h + 1) * HD]
                mixed = mixed + dot(weights.astype(jnp.bfloat16), values, ((1,), (0,)))
            out[:, cols] = (mixed / total).astype(jnp.bfloat16)


def cross(info, base, limit, parts, gain, weight, texts, heads, start, total_rows, done):
    pieces = len(parts)
    rows, piece = parts[0].shape
    width = weight.shape[1]
    whole = lambda shape: pl.BlockSpec(shape, lambda p, i: (0,) * len(shape))
    operands = [info, *parts, gain, weight, *texts]
    in_specs = [whole((rows, piece))] * pieces
    in_specs += [
        pl.BlockSpec((1, piece), lambda p, i: (0, p)),
        pl.BlockSpec((piece, width), lambda p, i: (i[base + p], 0)),
    ]
    in_specs += [whole(text.shape) for text in texts]
    aliases = {}
    if done is not None:
        aliases = {len(operands): 0}
        operands.append(done)
        in_specs.append(pl.BlockSpec(memory_space=pl.ANY))
    return pl.pallas_call(
        functools.partial(cross_body, heads, pieces, len(texts), limit),
        out_shape=jax.ShapeDtypeStruct((total_rows, width), jnp.bfloat16),
        grid_spec=pltpu.PrefetchScalarGridSpec(
            num_scalar_prefetch=1,
            grid=(pieces,),
            in_specs=in_specs,
            out_specs=pl.BlockSpec((rows, width), lambda p, i: (start // rows, 0)),
            scratch_shapes=[
                pltpu.VMEM((rows, 1), jnp.float32),
                pltpu.VMEM((rows, 1), jnp.float32),
                pltpu.VMEM((rows, width), jnp.float32),
            ],
        ),
        input_output_aliases=aliases,
        compiler_params=pltpu.CompilerParams(vmem_limit_bytes=CROSS_VMEM),
        name="cross",
    )(*operands)


def unpack_wide(x, width):
    return jnp.concatenate([x[:, n : n + width] for n in range(0, x.shape[1], width)])


def wide_unpack(x, count):
    return jnp.concatenate([x[n : n + count] for n in range(0, x.shape[0], count)], axis=1)


def after(value, *others):
    return lax.optimization_barrier((value, others))[0]


def self_line(info, left_check, query, key, value, heads, seq_size, right, left):
    same = lambda g: g
    pair = lambda k, v, check: ((k, same), (v, same), check)
    from_left = from_right = (key, value)
    state = attend(info, (query, same), [pair(key, value, None)], None, seq_size == 1, 1, heads)
    for step in range(1, seq_size):
        from_left = tuple(right(x) for x in from_left)
        from_right = tuple(left(x) for x in from_right)
        blocks = [
            pair(*from_left, left_check + 2 * (step - 1)),
            pair(*from_right, left_check + 2 * (step - 1) + 1),
        ]
        state = attend(info, (query, same), blocks, state, step == seq_size - 1, 1, heads)
    return state[0]


def text_line(text_part, square_part, place, seq_size, right, left):
    share = text_part.shape[0] // seq_size

    def rows_of(array, owner):
        return lax.dynamic_slice_in_dim(array, jnp.clip(owner, 0, seq_size - 1) * share, share)

    rightward = leftward = None
    for step in range(1, seq_size):
        ahead, behind = place + seq_size - step, place - seq_size + step
        to_right = rows_of(text_part, ahead), rows_of(square_part, ahead)
        to_left = rows_of(text_part, behind), rows_of(square_part, behind)
        if step > 1:
            to_right = tuple(a + b.astype(jnp.float32) for a, b in zip(to_right, rightward))
            to_left = tuple(a + b.astype(jnp.float32) for a, b in zip(to_left, leftward))
        rightward = right(to_right[0].astype(jnp.bfloat16), step), right(to_right[1], step)
        leftward = left(to_left[0].astype(jnp.bfloat16), step), left(to_left[1], step)
    text_sum, square_sum = (
        rows_of(own, place) + a.astype(jnp.float32) + b.astype(jnp.float32)
        for own, a, b in zip((text_part, square_part), rightward, leftward)
    )
    text_low = (text_sum / jnp.sqrt(square_sum / DT + 1e-06)[:, None]).astype(jnp.bfloat16)
    return lax.all_gather(text_low, "seq", axis=0, tiled=True)


def shards(
    seq_size,
    tensor_size,
    video_states,
    query_self,
    key_self,
    value_self,
    out_weight,
    cross_gain,
    query_weight,
    text_memory,
    text_gain,
    text_weight,
    prompt_length,
):
    local_rows, local_width = query_self.shape
    heads = local_width // HD
    place = lax.axis_index("seq")
    slot = lax.axis_index("tensor")
    paired = tensor_size == 4
    four = seq_size == 4 and heads == 6 and text_memory.shape[0] * 3 == local_rows * 4
    piece = cross_gain.shape[0]

    def right(x, most=seq_size):
        return lax.ppermute(x, "seq", [(n, n + 1) for n in range(min(most, seq_size - 1))])

    def left(x, most=seq_size):
        last = seq_size - 1
        return lax.ppermute(x, "seq", [(last - n, last - n - 1) for n in range(min(most, last))])

    def swap(x, bit):
        return lax.ppermute(x, "tensor", [(n, n ^ bit) for n in range(tensor_size)])

    is_end = (place == 0) | (place == seq_size - 1)
    if paired:
        order = [slot ^ 1, slot ^ 3, slot, slot ^ 2, slot ^ 1, slot ^ 3]
    else:
        order = [jnp.int32(n) for n in range(tensor_size)]
    scalars = [prompt_length[0], is_end, ~is_end] + order
    line_check = len(scalars)
    for step in range(1, seq_size):
        scalars += [place >= step, place + step < seq_size]
    info = jnp.stack([jnp.asarray(s).astype(jnp.int32) for s in scalars])
    LIMIT, END, MIDDLE, ORDER = 0, 1, 2, 3

    def text_parts(memory, gain, weight):
        memory_float = memory.astype(jnp.float32)
        scaled_text = (memory_float * gain).astype(jnp.bfloat16)
        square_part = jnp.sum(memory_float * memory_float, axis=1)
        text_part = jnp.dot(
            scaled_text, weight.reshape(weight.shape[0], -1), preferred_element_type=jnp.float32
        )
        return text_part, square_part

    if local_rows % 384 == 0:
        chunks = [(0, local_rows * 2 // 3), (local_rows * 2 // 3, local_rows // 3)]
    else:
        chunks = [(0, local_rows)]
    if four:
        def outer(x):
            return lax.ppermute(x, "seq", [(0, 1), (1, 0), (2, 3), (3, 2)])

        def inner(x):
            return lax.ppermute(x, "seq", [(0, 0), (1, 2), (2, 1), (3, 3)])

        cut = 2 * HD
        kept = lambda k, v, base, check: ((k, lambda g: g + base), (v, lambda g: g + base), check)
        lend = lambda k, v, check: ((k, lambda g: 0), (v, lambda g: 0), check)
        query_kept = (query_self, lambda g: g + 1)

        def fold(query, blocks, state, last=False):
            return attend(info, query, blocks, state, last, 2, 2)

        outer_1v, inner_1v = outer(value_self), inner(value_self)
        outer_1k, inner_1k = outer(key_self), inner(key_self)
        state = fold(query_kept, [kept(key_self, value_self, 1, None)], None)
        (text_memory, text_gain, text_weight, cross_gain, query_lent), state = lax.optimization_barrier(
            ((text_memory, text_gain, text_weight, cross_gain, query_self[:, :cut]), state)
        )
        text_part, square_part = text_parts(text_memory, text_gain, text_weight)
        text_low = text_part.astype(jnp.bfloat16)
        rows = text_part.shape[0]
        eighth = rows // 8

        def pack(start, stop):
            x = text_low[start * eighth : stop * eighth]
            width = x.shape[0] * x.shape[1] // local_rows
            return jnp.concatenate([x[:, n : n + width] for n in range(0, x.shape[1], width)])

        def unpack(x, count):
            count = count * eighth
            return jnp.concatenate([x[n : n + count] for n in range(0, x.shape[0], count)], axis=1)

        inner_2v = inner(outer_1v)
        query_pack = jnp.concatenate([query_lent, pack(2, 3)], axis=1)
        given = jnp.where(is_end, query_pack, inner_1v[:, cut:])
        outer_2v = outer(given)
        inner_2k = inner(outer_1k)
        outer_2k = outer(jnp.where(is_end, pack(0, 2), inner_1k[:, cut:]))
        state = fold(query_kept, [kept(outer_1k, outer_1v, 1, None), kept(inner_1k, inner_1v, 1, MIDDLE)], state)
        outer_3v = outer(jnp.where(is_end, pack(3, 5), inner_2v[:, cut:]))
        both_lent = (jnp.concatenate([query_lent, outer_2v[:, :cut]], axis=1), lambda g: g)
        loan = fold(
            both_lent,
            [lend(key_self, value_self, None), lend(outer_1k, outer_1v, MIDDLE), lend(inner_1k, inner_1v, MIDDLE)],
            None,
        )
        text_sums, text_others, start = [], [], 0

        def add_text(*parts):
            rows = sum(part.shape[0] for part in parts)
            part = jnp.concatenate(parts) if len(parts) > 1 else parts[0]
            part = after(part, *text_sums)
            own = lax.optimization_barrier(text_part[start : start + rows] + part.astype(jnp.float32))
            text_sums.append(own)
            text_others.append(inner(own.astype(jnp.bfloat16)))
            return start + rows

        start = add_text(unpack(outer_2k, 2), unpack(outer_2v[:, cut:], 1))
        outer_3k = outer(jnp.where(is_end, pack(5, 7), inner_2k[:, cut:]))
        square_sum = square_part + outer(square_part)
        loan = fold(both_lent, [lend(inner_2k, inner_2v, MIDDLE)], loan, True)[0]
        given = jnp.where(is_end, unpack_wide(text_low[7 * eighth :], loan.shape[1]), loan[cut:])
        back = outer(given)
        root = jnp.sqrt((square_sum + inner(square_sum)) / DT + 1e-06)
        state = fold(query_kept, [kept(outer_2k, outer_2v, 0, END), kept(inner_2k, inner_2v, 1, MIDDLE)], state)
        start = add_text(unpack(outer_3v, 2))
        rest = fold(query_kept, [kept(outer_3k, outer_3v, 0, END)], state, True)[0]
        mixed = [loan[:cut], back, rest]
        mixed_check = END
    else:
        mixed = [self_line(info, line_check, query_self, key_self, value_self, heads, seq_size, right, left)]
        mixed_check = None
        text_part, square_part = text_parts(text_memory, text_gain, text_weight)
        texts = [text_line(text_part, square_part, place, seq_size, right, left)]

    if paired:
        gain_two = jnp.stack([cross_gain, swap(cross_gain, 2)])
        gain_all = jnp.concatenate([gain_two, swap(gain_two, 1)]).reshape(1, -1)
        overs, mines, sents = [], [], []
        for start_row, rows in chunks:
            spot = (mixed_check, start_row, rows, out_weight, tensor_size)
            theirs = project(info, mixed, *spot, ORDER, 2)
            sent = after(swap(theirs, 1), *overs)
            own = project(info, mixed, *spot, ORDER + 2, 2)
            total = own[:, piece:].astype(jnp.float32) + sent[:, piece:].astype(jnp.float32)
            overs.append(total.astype(jnp.bfloat16))
            mines.append(own)
            sents.append(sent)
        others = [swap(x, 2) for x in overs]
    else:
        gain_all = lax.all_gather(cross_gain, "tensor", axis=0, tiled=True).reshape(1, -1)
        partials = [
            project(info, mixed, mixed_check, start_row, rows, out_weight, tensor_size, ORDER, tensor_size)
            for start_row, rows in chunks
        ]
    if four:
        add_text(unpack(outer_3k, 2), wide_unpack(back, eighth))
        texts = []
        start = 0
        for own, other in zip(text_sums, text_others):
            share = root[start : start + own.shape[0]]
            start += own.shape[0]
            total = ((own + other.astype(jnp.float32)) / share[:, None]).astype(jnp.bfloat16)
            texts.append(jnp.where(is_end, outer(total), total))
    out, residuals = None, []
    for n, (start_row, rows) in enumerate(chunks):
        video = video_states[start_row : start_row + rows].astype(jnp.float32)
        if paired:
            residual = (
                video
                + mines[n][:, :piece].astype(jnp.float32)
                + sents[n][:, :piece].astype(jnp.float32)
                + after(others[n], *residuals).astype(jnp.float32)
            ).astype(jnp.bfloat16)
            across = swap(residual, 2)
            parts = [residual, across, swap(residual, 1), swap(across, 1)]
            base = ORDER + 2
        else:
            summed = lax.psum_scatter(partials[n], "tensor", scatter_dimension=1, tiled=True)
            residual = (video + summed.astype(jnp.float32)).astype(jnp.bfloat16)
            gathered = lax.all_gather(residual, "tensor", axis=1, tiled=True)
            parts = [gathered[:, m * piece : (m + 1) * piece] for m in range(tensor_size)]
            base = ORDER
        residuals.append(residual)
        spot = (start_row, local_rows, out)
        out = cross(info, base, LIMIT, parts, gain_all, query_weight, texts, heads, *spot)
    return (jnp.concatenate(residuals), out)


def solution(mesh):
    in_specs = (
        P(("groups", "seq"), "tensor"),
        P(("groups", "seq"), "tensor"),
        P(("groups", "seq"), "tensor"),
        P(("groups", "seq"), "tensor"),
        P("tensor", None),
        P("tensor"),
        P(None, "tensor"),
        P("groups", "seq"),
        P("seq"),
        P("seq", None, "tensor"),
        P("groups"),
    )
    out_specs = (P(("groups", "seq"), "tensor"), P(("groups", "seq"), "tensor"))

    def body(*args):
        return shards(mesh.shape["seq"], mesh.shape["tensor"], *args)

    return jax.shard_map(body, mesh=mesh, in_specs=in_specs, out_specs=out_specs, check_vma=False)
```

```python
import functools
import math

import jax
import jax.numpy as jnp
from jax import lax
from jax.experimental import pallas as pl
from jax.experimental.pallas import tpu as pltpu
from jax.sharding import PartitionSpec as P


D = 5120
DT = 4096
HD = 128
FACTOR = 1.0 / math.sqrt(HD)
EXP2 = FACTOR * math.log2(math.e)

ATTEND_VMEM = 16 << 20
PROJECT_VMEM = 24 << 20
CROSS_VMEM = 28 << 20


def dot(a, b, dims):
    return lax.dot_general(a, b, (dims, ((), ())), preferred_element_type=jnp.float32)


def attend_body(per, checks, first, last, info, query, *refs):
    count = len(checks)
    blocks = refs[: 2 * count]
    refs = refs[2 * count :]
    if not first:
        stat_in, acc_in = refs[:2]
        refs = refs[2:]
    outs, (stat, acc) = refs[:-2], refs[-2:]
    if not first:
        stat[...] = stat_in[...]
        acc[...] = acc_in[...]
    for n, check in enumerate(checks):
        key, value = blocks[2 * n], blocks[2 * n + 1]
        fresh = first and n == 0

        def fold(key=key, value=value, fresh=fresh):
            for h in range(per):
                cols = slice(h * HD, (h + 1) * HD)
                top_row, sum_row = slice(8 * h, 8 * h + 1), slice(8 * h + 1, 8 * h + 2)
                scores = dot(key[:, cols], query[:, cols], ((1,), (1,)))
                top = jnp.max(scores, axis=0, keepdims=True)
                if not fresh:
                    old = stat[top_row, :]
                    top = jnp.maximum(old, top)
                weights = jnp.exp2((scores - top) * EXP2)
                total = jnp.sum(weights, axis=0, keepdims=True)
                mixed = dot(value[:, cols], weights.astype(jnp.bfloat16), ((0,), (0,)))
                if not fresh:
                    shrink = jnp.exp2((old - top) * EXP2)
                    total = total + stat[sum_row, :] * shrink
                    mixed = mixed + acc[cols, :] * shrink
                stat[top_row, :] = top
                stat[sum_row, :] = total
                acc[cols, :] = mixed

        if check is None:
            fold()
        else:
            pl.when(info[check] > 0)(fold)
    if last:
        for h in range(per):
            cols = slice(h * HD, (h + 1) * HD)
            outs[0][cols, :] = (acc[cols, :] / stat[8 * h + 1 : 8 * h + 2, :]).astype(jnp.bfloat16)
    else:
        outs[0][...] = stat[...]
        outs[1][...] = acc[...]


def attend(info, query, blocks, state, last, per, groups):
    rows = query[0].shape[0]
    first = state is None

    def spec(pair):
        array, index = pair
        return pl.BlockSpec((array.shape[0], per * HD), lambda g, i: (0, index(g)))

    in_specs = [spec(query)]
    operands = [query[0]]
    for key, value, check in blocks:
        in_specs += [spec(key), spec(value)]
        operands += [key[0], value[0]]
    stat_spec = pl.BlockSpec((8 * per, rows), lambda g, i: (g, 0))
    acc_spec = pl.BlockSpec((HD * per, rows), lambda g, i: (g, 0))
    if not first:
        in_specs += [stat_spec, acc_spec]
        operands += list(state)
    width = HD * per * groups
    if last:
        out_shape = [jax.ShapeDtypeStruct((width, rows), jnp.bfloat16)]
        out_specs = [acc_spec]
    else:
        out_shape = [
            jax.ShapeDtypeStruct((8 * per * groups, rows), jnp.float32),
            jax.ShapeDtypeStruct((width, rows), jnp.float32),
        ]
        out_specs = [stat_spec, acc_spec]
    return pl.pallas_call(
        functools.partial(attend_body, per, [b[2] for b in blocks], first, last),
        out_shape=out_shape,
        grid_spec=pltpu.PrefetchScalarGridSpec(
            num_scalar_prefetch=1,
            grid=(groups,),
            in_specs=in_specs,
            out_specs=out_specs,
            scratch_shapes=[
                pltpu.VMEM((8 * per, rows), jnp.float32),
                pltpu.VMEM((HD * per, rows), jnp.float32),
            ],
        ),
        compiler_params=pltpu.CompilerParams(vmem_limit_bytes=ATTEND_VMEM),
        name="attend",
    )(info, *operands)


def trim_body(cut, key, value, key_kept, value_kept, sems):
    rest = pl.ds(cut, key_kept.shape[1])
    pairs = [
        (value.at[:, rest], value_kept),
        (key.at[:, rest], key_kept),
    ]
    copies = [pltpu.make_async_copy(*pair, sems.at[n]) for n, pair in enumerate(pairs)]
    for copy in copies:
        copy.start()
    for copy in copies:
        copy.wait()


def trim(key, value, cut):
    rows, width = key.shape
    kept = jax.ShapeDtypeStruct((rows, width - cut), key.dtype)
    return pl.pallas_call(
        functools.partial(trim_body, cut),
        out_shape=[kept, kept],
        in_specs=[pl.BlockSpec(memory_space=pl.ANY)] * 2,
        out_specs=[pl.BlockSpec(memory_space=pl.ANY)] * 2,
        scratch_shapes=[pltpu.SemaphoreType.DMA((2,))],
        compiler_params=pltpu.CompilerParams(vmem_limit_bytes=ATTEND_VMEM),
        name="trim",
    )(key, value)


def project_body(check, info, *refs):
    mixed, weight, out = refs[:-2], refs[-2], refs[-1]
    if check is None:
        total = dot(mixed[0][...], weight[...], ((0,), (0,)))
    else:
        near, far, rest = mixed
        lead = jnp.where(info[check] > 0, far[...], near[...])
        cut = lead.shape[0]
        total = dot(lead, weight[:cut, :], ((0,), (0,))) + dot(rest[...], weight[cut:, :], ((0,), (0,)))
    out[...] = total.astype(jnp.bfloat16)


def project(info, mixed, check, start, rows, weight, pieces, base, count):
    piece = weight.shape[1] // pieces
    return pl.pallas_call(
        functools.partial(project_body, check),
        out_shape=jax.ShapeDtypeStruct((rows, piece * count), jnp.bfloat16),
        grid_spec=pltpu.PrefetchScalarGridSpec(
            num_scalar_prefetch=1,
            grid=(count,),
            in_specs=[pl.BlockSpec((m.shape[0], rows), lambda p, i: (0, start // rows)) for m in mixed]
            + [pl.BlockSpec((weight.shape[0], piece), lambda p, i: (0, i[base + p]))],
            out_specs=pl.BlockSpec((rows, piece), lambda p, i: (0, p)),
        ),
        compiler_params=pltpu.CompilerParams(vmem_limit_bytes=PROJECT_VMEM),
        name="project",
    )(info, *mixed, weight)


def normed_query(info, base, parts, gain, weight):
    piece = parts[0].shape[1]
    total = 0.0
    squares = 0.0
    for part in parts:
        value = part[...].astype(jnp.float32)
        total = total + jnp.sum(value, axis=1, keepdims=True)
        squares = squares + jnp.sum(value * value, axis=1, keepdims=True)
    mean = total / D
    scale = lax.rsqrt(squares / D - mean * mean + 1e-06)
    acc = 0.0
    for n, part in enumerate(parts):
        value = part[...].astype(jnp.float32)
        normed = ((value - mean) * scale * gain[:, n * piece : (n + 1) * piece]).astype(jnp.bfloat16)
        spot = pl.ds(pl.multiple_of(info[base + n] * piece, piece), piece)
        acc = acc + dot(normed, weight[spot, :], ((1,), (0,)))
    return acc.astype(jnp.bfloat16)


def answer(query, texts, length, block):
    width = block.shape[1]
    for h in range(width // HD):
        cols = slice(h * HD, (h + 1) * HD)
        total = 0.0
        mixed = 0.0
        first = 0
        for text in texts:
            token = first + lax.broadcasted_iota(jnp.int32, (1, text.shape[0]), 1)
            first += text.shape[0]
            scores = dot(query[:, cols], text[:, cols], ((1,), (1,))) * FACTOR
            weights = jnp.exp(jnp.where(token < length, scores, -1e30))
            total = total + jnp.sum(weights, axis=1, keepdims=True)
            values = text[:, width + h * HD : width + (h + 1) * HD]
            mixed = mixed + dot(weights.astype(jnp.bfloat16), values, ((1,), (0,)))
        block[:, cols] = (mixed / total).astype(jnp.bfloat16)


def query_body(pieces, base, info, *refs):
    parts, (gain, weight, out) = refs[:pieces], refs[pieces:]
    out[...] = normed_query(info, base, parts, gain, weight)


def cross_body(pieces, count, base, limit, start, info, *refs):
    texts, refs = refs[:count], refs[count:]
    out, block, sem = refs[-3:]
    if pieces:
        query = normed_query(info, base, refs[:pieces], refs[pieces], refs[pieces + 1])
    else:
        query = refs[0][...]
    answer(query, texts, info[limit], block)
    copy = pltpu.make_async_copy(block, out.at[pl.ds(start, block.shape[0]), :], sem)
    copy.start()
    copy.wait()


def cross_query(info, base, parts, gain, weight):
    operands = [*parts, gain, weight]
    in_specs = [pl.BlockSpec(memory_space=pltpu.SMEM)]
    return pl.pallas_call(
        functools.partial(query_body, len(parts), base),
        out_shape=jax.ShapeDtypeStruct((parts[0].shape[0], weight.shape[1]), jnp.bfloat16),
        in_specs=in_specs + [pl.BlockSpec(memory_space=pltpu.VMEM)] * len(operands),
        out_specs=pl.BlockSpec(memory_space=pltpu.VMEM),
        compiler_params=pltpu.CompilerParams(vmem_limit_bytes=CROSS_VMEM),
        name="query",
    )(info, *operands)


def cross(info, base, limit, texts, sources, width, start, total_rows, done):
    rows = sources[0].shape[0]
    pieces = len(sources) - 2 if len(sources) > 1 else 0
    operands = [info, *texts, *sources]
    in_specs = [pl.BlockSpec(memory_space=pltpu.SMEM)]
    in_specs += [pl.BlockSpec(memory_space=pltpu.VMEM)] * (len(operands) - 1)
    aliases = {}
    if done is not None:
        aliases = {len(operands): 0}
        operands.append(done)
        in_specs.append(pl.BlockSpec(memory_space=pl.ANY))
    return pl.pallas_call(
        functools.partial(cross_body, pieces, len(texts), base, limit, start),
        out_shape=jax.ShapeDtypeStruct((total_rows, width), jnp.bfloat16),
        in_specs=in_specs,
        out_specs=pl.BlockSpec(memory_space=pl.ANY),
        scratch_shapes=[pltpu.VMEM((rows, width), jnp.bfloat16), pltpu.SemaphoreType.DMA(())],
        input_output_aliases=aliases,
        compiler_params=pltpu.CompilerParams(vmem_limit_bytes=CROSS_VMEM),
        name="cross",
    )(*operands)


def unpack_wide(x, width):
    return jnp.concatenate([x[:, n : n + width] for n in range(0, x.shape[1], width)])


def wide_unpack(x, count):
    return jnp.concatenate([x[n : n + count] for n in range(0, x.shape[0], count)], axis=1)


def after(value, *others):
    return lax.optimization_barrier((value, others))[0]


def self_line(info, left_check, query, key, value, heads, seq_size, right, left):
    same = lambda g: g
    pair = lambda k, v, check: ((k, same), (v, same), check)
    from_left = from_right = (key, value)
    state = attend(info, (query, same), [pair(key, value, None)], None, seq_size == 1, 1, heads)
    for step in range(1, seq_size):
        from_left = tuple(right(x) for x in from_left)
        from_right = tuple(left(x) for x in from_right)
        blocks = [
            pair(*from_left, left_check + 2 * (step - 1)),
            pair(*from_right, left_check + 2 * (step - 1) + 1),
        ]
        state = attend(info, (query, same), blocks, state, step == seq_size - 1, 1, heads)
    return state[0]


def text_line(text_part, square_part, place, seq_size, right, left):
    share = text_part.shape[0] // seq_size

    def rows_of(array, owner):
        return lax.dynamic_slice_in_dim(array, jnp.clip(owner, 0, seq_size - 1) * share, share)

    rightward = leftward = None
    for step in range(1, seq_size):
        ahead, behind = place + seq_size - step, place - seq_size + step
        to_right = rows_of(text_part, ahead), rows_of(square_part, ahead)
        to_left = rows_of(text_part, behind), rows_of(square_part, behind)
        if step > 1:
            to_right = tuple(a + b.astype(jnp.float32) for a, b in zip(to_right, rightward))
            to_left = tuple(a + b.astype(jnp.float32) for a, b in zip(to_left, leftward))
        rightward = right(to_right[0].astype(jnp.bfloat16), step), right(to_right[1], step)
        leftward = left(to_left[0].astype(jnp.bfloat16), step), left(to_left[1], step)
    text_sum, square_sum = (
        rows_of(own, place) + a.astype(jnp.float32) + b.astype(jnp.float32)
        for own, a, b in zip((text_part, square_part), rightward, leftward)
    )
    text_low = (text_sum / jnp.sqrt(square_sum / DT + 1e-06)[:, None]).astype(jnp.bfloat16)
    return lax.all_gather(text_low, "seq", axis=0, tiled=True)


def shards(
    seq_size,
    tensor_size,
    video_states,
    query_self,
    key_self,
    value_self,
    out_weight,
    cross_gain,
    query_weight,
    text_memory,
    text_gain,
    text_weight,
    prompt_length,
):
    local_rows, local_width = query_self.shape
    heads = local_width // HD
    place = lax.axis_index("seq")
    slot = lax.axis_index("tensor")
    paired = tensor_size == 4
    four = seq_size == 4 and heads == 6 and text_memory.shape[0] * 3 == local_rows * 4
    piece = cross_gain.shape[0]

    def right(x, most=seq_size):
        return lax.ppermute(x, "seq", [(n, n + 1) for n in range(min(most, seq_size - 1))])

    def left(x, most=seq_size):
        last = seq_size - 1
        return lax.ppermute(x, "seq", [(last - n, last - n - 1) for n in range(min(most, last))])

    def swap(x, bit):
        return lax.ppermute(x, "tensor", [(n, n ^ bit) for n in range(tensor_size)])

    is_end = (place == 0) | (place == seq_size - 1)
    if paired:
        order = [slot ^ 1, slot ^ 3, slot, slot ^ 2, slot ^ 1, slot ^ 3]
    else:
        order = [jnp.int32(n) for n in range(tensor_size)]
    scalars = [prompt_length[0], is_end, ~is_end] + order
    line_check = len(scalars)
    for step in range(1, seq_size):
        scalars += [place >= step, place + step < seq_size]
    info = jnp.stack([jnp.asarray(s).astype(jnp.int32) for s in scalars])
    LIMIT, END, MIDDLE, ORDER = 0, 1, 2, 3

    def text_parts(memory, gain, weight):
        memory_float = memory.astype(jnp.float32)
        scaled_text = (memory_float * gain).astype(jnp.bfloat16)
        square_part = jnp.sum(memory_float * memory_float, axis=1)
        text_part = jnp.dot(
            scaled_text, weight.reshape(weight.shape[0], -1), preferred_element_type=jnp.float32
        )
        return text_part, square_part

    if local_rows % 384 == 0:
        chunks = [(0, local_rows * 2 // 3), (local_rows * 2 // 3, local_rows // 3)]
    else:
        chunks = [(0, local_rows)]
    if four:
        def outer(x):
            return lax.ppermute(x, "seq", [(0, 1), (1, 0), (2, 3), (3, 2)])

        def inner(x):
            return lax.ppermute(x, "seq", [(0, 0), (1, 2), (2, 1), (3, 3)])

        cut = 2 * HD
        kept = lambda k, v, base, check: ((k, lambda g: g + base), (v, lambda g: g + base), check)
        lend = lambda k, v, check: ((k, lambda g: 0), (v, lambda g: 0), check)
        query_kept = (query_self, lambda g: g + 1)

        def fold(query, blocks, state, last=False):
            return attend(info, query, blocks, state, last, 2, 2)

        inner_1v, inner_1k = inner(value_self), inner(key_self)
        kept_k, kept_v = trim(key_self, value_self, cut)
        outer_1v, outer_1k = outer(kept_v), outer(kept_k)
        state = fold(query_kept, [kept(key_self, value_self, 1, None)], None)
        (text_memory, text_gain, text_weight, cross_gain), state = lax.optimization_barrier(
            ((text_memory, text_gain, text_weight, cross_gain), state)
        )
        query_lent = query_self[:, :cut]
        text_part, square_part = text_parts(text_memory, text_gain, text_weight)
        text_low = text_part.astype(jnp.bfloat16)
        rows = text_part.shape[0]
        eighth = rows // 8

        def pack(start, stop):
            x = text_low[start * eighth : stop * eighth]
            width = x.shape[0] * x.shape[1] // local_rows
            return jnp.concatenate([x[:, n : n + width] for n in range(0, x.shape[1], width)])

        def unpack(x, count):
            count = count * eighth
            return jnp.concatenate([x[n : n + count] for n in range(0, x.shape[0], count)], axis=1)

        inner_2v = inner(outer_1v)
        given = jnp.where(is_end, jnp.concatenate([key_self[:, :cut], value_self[:, :cut]], axis=1), inner_1v[:, cut:])
        outer_2v = outer(given)
        inner_2k = inner(outer_1k)
        query_pack = jnp.concatenate([query_lent, pack(0, 1)], axis=1)
        given = jnp.where(is_end, query_pack, inner_1k[:, cut:])
        outer_2k = outer(given)
        square_sum = square_part + outer(square_part)
        state = fold(
            query_kept, [kept(outer_1k, outer_1v, 0, None), kept(inner_1k, inner_1v, 1, MIDDLE)], state
        )
        inner_2a = inner(outer_2v)
        outer_3v = outer(jnp.where(is_end, pack(1, 3), inner_2v))
        both_lent = (jnp.concatenate([query_lent, outer_2k[:, :cut]], axis=1), lambda g: g)
        near = ((outer_2v, lambda g: 0), (outer_2v, lambda g: 1), MIDDLE)
        far = ((inner_2a, lambda g: 0), (inner_2a, lambda g: 1), MIDDLE)
        loan = fold(
            both_lent,
            [lend(key_self, value_self, None), near, lend(inner_1k, inner_1v, MIDDLE)],
            None,
        )
        outer_3k = outer(jnp.where(is_end, pack(3, 5), inner_2k))
        loan = fold(both_lent, [far], loan, True)[0]
        given = jnp.where(
            is_end, unpack_wide(text_low[5 * eighth : 6 * eighth], loan.shape[1]), loan[cut:]
        )
        back = outer(given)
        text_sums, text_others, start = [], [], 0

        def add_text(*parts):
            rows = sum(part.shape[0] for part in parts)
            part = jnp.concatenate(parts) if len(parts) > 1 else parts[0]
            part = after(part, *text_sums)
            own = lax.optimization_barrier(text_part[start : start + rows] + part.astype(jnp.float32))
            text_sums.append(own)
            text_others.append(inner(own.astype(jnp.bfloat16)))
            return start + rows

        start = add_text(unpack(outer_2k[:, cut:], 1), unpack(outer_3v, 2))
        root = jnp.sqrt((square_sum + inner(square_sum)) / DT + 1e-06)
        state = fold(
            query_kept, [kept(outer_2k, outer_2v, 0, END), kept(inner_2k, inner_2v, 0, MIDDLE)], state
        )
        rest = fold(query_kept, [kept(outer_3k, outer_3v, 0, END)], state, True)[0]
        mixed = [loan[:cut], back, rest]
        mixed_check = END
    else:
        mixed = [self_line(info, line_check, query_self, key_self, value_self, heads, seq_size, right, left)]
        mixed_check = None
        text_part, square_part = text_parts(text_memory, text_gain, text_weight)
        texts = [text_line(text_part, square_part, place, seq_size, right, left)]

    if paired:
        gain_two = jnp.stack([cross_gain, swap(cross_gain, 2)])
        gain_all = jnp.concatenate([gain_two, swap(gain_two, 1)]).reshape(1, -1)
        overs, mines, sents = [], [], []
        for start_row, rows in chunks:
            spot = (mixed_check, start_row, rows, out_weight, tensor_size)
            theirs = project(info, mixed, *spot, ORDER, 2)
            sent = after(swap(theirs, 1), *overs)
            own = project(info, mixed, *spot, ORDER + 2, 2)
            total = own[:, piece:].astype(jnp.float32) + sent[:, piece:].astype(jnp.float32)
            overs.append(total.astype(jnp.bfloat16))
            mines.append(own)
            sents.append(sent)
        others = [swap(x, 2) for x in overs]
    else:
        gain_all = lax.all_gather(cross_gain, "tensor", axis=0, tiled=True).reshape(1, -1)
        partials = [
            project(info, mixed, mixed_check, start_row, rows, out_weight, tensor_size, ORDER, tensor_size)
            for start_row, rows in chunks
        ]
    if four:
        start = add_text(unpack(outer_3k, 2), wide_unpack(back, eighth))
        texts, row = [], 0
        for n in range(3):
            own, other = text_sums[n], text_others[n]
            share = root[row : row + own.shape[0]]
            row += own.shape[0]
            total = ((own + other.astype(jnp.float32)) / share[:, None]).astype(jnp.bfloat16)
            given = jnp.where(is_end, text_low[5 * eighth :], total) if n == 0 else total
            taken = outer(given)
            texts.append(jnp.where(is_end, taken, total))
            if n == 0:
                add_text(taken[eighth:])
    out, residuals = None, []
    for n, (start_row, rows) in enumerate(chunks):
        video = video_states[start_row : start_row + rows].astype(jnp.float32)
        if paired:
            residual = (
                video
                + mines[n][:, :piece].astype(jnp.float32)
                + sents[n][:, :piece].astype(jnp.float32)
                + after(others[n], *residuals).astype(jnp.float32)
            ).astype(jnp.bfloat16)
            across = swap(residual, 2)
            parts = [residual, across, swap(residual, 1), swap(across, 1)]
            base = ORDER + 2
        else:
            summed = lax.psum_scatter(partials[n], "tensor", scatter_dimension=1, tiled=True)
            residual = (video + summed.astype(jnp.float32)).astype(jnp.bfloat16)
            gathered = lax.all_gather(residual, "tensor", axis=1, tiled=True)
            parts = [gathered[:, m * piece : (m + 1) * piece] for m in range(tensor_size)]
            base = ORDER
        residuals.append(residual)
        sources = [*parts, gain_all, query_weight]
        if n < len(chunks) - 1:
            sources = [cross_query(info, base, *(parts, gain_all, query_weight))]
        spot = (local_width, start_row, local_rows, out)
        out = cross(info, base, LIMIT, texts, sources, *spot)
    return (jnp.concatenate(residuals), out)


def solution(mesh):
    in_specs = (
        P(("groups", "seq"), "tensor"),
        P(("groups", "seq"), "tensor"),
        P(("groups", "seq"), "tensor"),
        P(("groups", "seq"), "tensor"),
        P("tensor", None),
        P("tensor"),
        P(None, "tensor"),
        P("groups", "seq"),
        P("seq"),
        P("seq", None, "tensor"),
        P("groups"),
    )
    out_specs = (P(("groups", "seq"), "tensor"), P(("groups", "seq"), "tensor"))

    def body(*args):
        return shards(mesh.shape["seq"], mesh.shape["tensor"], *args)

    return jax.shard_map(body, mesh=mesh, in_specs=in_specs, out_specs=out_specs, check_vma=False)
```

```python
import functools
import math

import jax
import jax.numpy as jnp
from jax import lax
from jax.experimental import pallas as pl
from jax.experimental.pallas import tpu as pltpu
from jax.sharding import PartitionSpec as P


D = 5120
DT = 4096
HD = 128
FACTOR = 1.0 / math.sqrt(HD)
EXP2 = FACTOR * math.log2(math.e)

ATTEND_VMEM = 16 << 20
PROJECT_VMEM = 24 << 20
CROSS_VMEM = 28 << 20


def dot(a, b, dims):
    return lax.dot_general(a, b, (dims, ((), ())), preferred_element_type=jnp.float32)


def attend_body(per, checks, first, last, info, query, *refs):
    count = len(checks)
    blocks = refs[: 2 * count]
    refs = refs[2 * count :]
    if not first:
        stat_in, acc_in = refs[:2]
        refs = refs[2:]
    outs, (stat, acc) = refs[:-2], refs[-2:]
    if not first:
        stat[...] = stat_in[...]
        acc[...] = acc_in[...]
    for n, check in enumerate(checks):
        key, value = blocks[2 * n], blocks[2 * n + 1]
        fresh = first and n == 0

        def fold(key=key, value=value, fresh=fresh):
            for h in range(per):
                cols = slice(h * HD, (h + 1) * HD)
                top_row, sum_row = slice(8 * h, 8 * h + 1), slice(8 * h + 1, 8 * h + 2)
                scores = dot(key[:, cols], query[:, cols], ((1,), (1,)))
                top = jnp.max(scores, axis=0, keepdims=True)
                if not fresh:
                    old = stat[top_row, :]
                    top = jnp.maximum(old, top)
                weights = jnp.exp2((scores - top) * EXP2)
                total = jnp.sum(weights, axis=0, keepdims=True)
                mixed = dot(value[:, cols], weights.astype(jnp.bfloat16), ((0,), (0,)))
                if not fresh:
                    shrink = jnp.exp2((old - top) * EXP2)
                    total = total + stat[sum_row, :] * shrink
                    mixed = mixed + acc[cols, :] * shrink
                stat[top_row, :] = top
                stat[sum_row, :] = total
                acc[cols, :] = mixed

        if check is None:
            fold()
        else:
            pl.when(info[check] > 0)(fold)
    if last:
        for h in range(per):
            cols = slice(h * HD, (h + 1) * HD)
            outs[0][cols, :] = (acc[cols, :] / stat[8 * h + 1 : 8 * h + 2, :]).astype(jnp.bfloat16)
    else:
        outs[0][...] = stat[...]
        outs[1][...] = acc[...]


def attend(info, query, blocks, state, last, per, groups):
    rows = query[0].shape[0]
    first = state is None

    def spec(pair):
        array, index = pair
        return pl.BlockSpec((array.shape[0], per * HD), lambda g, i: (0, index(g)))

    in_specs = [spec(query)]
    operands = [query[0]]
    for key, value, check in blocks:
        in_specs += [spec(key), spec(value)]
        operands += [key[0], value[0]]
    stat_spec = pl.BlockSpec((8 * per, rows), lambda g, i: (g, 0))
    acc_spec = pl.BlockSpec((HD * per, rows), lambda g, i: (g, 0))
    if not first:
        in_specs += [stat_spec, acc_spec]
        operands += list(state)
    width = HD * per * groups
    if last:
        out_shape = [jax.ShapeDtypeStruct((width, rows), jnp.bfloat16)]
        out_specs = [acc_spec]
    else:
        out_shape = [
            jax.ShapeDtypeStruct((8 * per * groups, rows), jnp.float32),
            jax.ShapeDtypeStruct((width, rows), jnp.float32),
        ]
        out_specs = [stat_spec, acc_spec]
    return pl.pallas_call(
        functools.partial(attend_body, per, [b[2] for b in blocks], first, last),
        out_shape=out_shape,
        grid_spec=pltpu.PrefetchScalarGridSpec(
            num_scalar_prefetch=1,
            grid=(groups,),
            in_specs=in_specs,
            out_specs=out_specs,
            scratch_shapes=[
                pltpu.VMEM((8 * per, rows), jnp.float32),
                pltpu.VMEM((HD * per, rows), jnp.float32),
            ],
        ),
        compiler_params=pltpu.CompilerParams(vmem_limit_bytes=ATTEND_VMEM),
        name="attend",
    )(info, *operands)


def trim_body(cut, key, value, key_kept, value_kept, sems):
    rest = pl.ds(cut, key_kept.shape[1])
    pairs = [
        (value.at[:, rest], value_kept),
        (key.at[:, rest], key_kept),
    ]
    copies = [pltpu.make_async_copy(*pair, sems.at[n]) for n, pair in enumerate(pairs)]
    for copy in copies:
        copy.start()
    for copy in copies:
        copy.wait()


def trim(key, value, cut):
    rows, width = key.shape
    kept = jax.ShapeDtypeStruct((rows, width - cut), key.dtype)
    return pl.pallas_call(
        functools.partial(trim_body, cut),
        out_shape=[kept, kept],
        in_specs=[pl.BlockSpec(memory_space=pl.ANY)] * 2,
        out_specs=[pl.BlockSpec(memory_space=pl.ANY)] * 2,
        scratch_shapes=[pltpu.SemaphoreType.DMA((2,))],
        compiler_params=pltpu.CompilerParams(vmem_limit_bytes=ATTEND_VMEM),
        name="trim",
    )(key, value)


def project_body(check, info, *refs):
    mixed, weight, out = refs[:-2], refs[-2], refs[-1]
    if check is None:
        total = dot(mixed[0][...], weight[...], ((0,), (0,)))
    else:
        near, far, rest = mixed
        lead = jnp.where(info[check] > 0, far[...], near[...])
        cut = lead.shape[0]
        total = dot(lead, weight[:cut, :], ((0,), (0,))) + dot(rest[...], weight[cut:, :], ((0,), (0,)))
    out[...] = total.astype(jnp.bfloat16)


def project(info, mixed, check, start, rows, weight, pieces, base, count):
    piece = weight.shape[1] // pieces
    return pl.pallas_call(
        functools.partial(project_body, check),
        out_shape=jax.ShapeDtypeStruct((rows, piece * count), jnp.bfloat16),
        grid_spec=pltpu.PrefetchScalarGridSpec(
            num_scalar_prefetch=1,
            grid=(count,),
            in_specs=[pl.BlockSpec((m.shape[0], rows), lambda p, i: (0, start // rows)) for m in mixed]
            + [pl.BlockSpec((weight.shape[0], piece), lambda p, i: (0, i[base + p]))],
            out_specs=pl.BlockSpec((rows, piece), lambda p, i: (0, p)),
        ),
        compiler_params=pltpu.CompilerParams(vmem_limit_bytes=PROJECT_VMEM),
        name="project",
    )(info, *mixed, weight)


def centred(info, base, which, parts, center, gain, weight):
    piece = parts[0].shape[1]
    acc = 0.0
    for n, part in zip(which, parts):
        value = part[...].astype(jnp.float32)
        value = ((value - center) * gain[:, n * piece : (n + 1) * piece]).astype(jnp.bfloat16)
        spot = pl.ds(pl.multiple_of(info[base + n] * piece, piece), piece)
        acc = acc + dot(value, weight[spot, :], ((1,), (0,)))
    return acc


def row_sums(parts):
    total = squares = 0.0
    for part in parts:
        value = part[...].astype(jnp.float32)
        total = total + jnp.sum(value, axis=1, keepdims=True)
        squares = squares + jnp.sum(value * value, axis=1, keepdims=True)
    return total, squares


def gain_body(base, pieces, info, gain, weight, out):
    piece = gain.shape[1] // pieces
    row = lax.broadcasted_iota(jnp.int32, (16, piece), 0)
    acc = 0.0
    for n in range(pieces):
        whole = gain[:, n * piece : (n + 1) * piece]
        high = whole.astype(jnp.bfloat16).astype(jnp.float32)
        both = jnp.where(row == 0, high, jnp.where(row == 1, whole - high, 0.0)).astype(jnp.bfloat16)
        spot = pl.ds(pl.multiple_of(info[base + n] * piece, piece), piece)
        acc = acc + dot(both, weight[spot, :], ((1,), (0,)))
    out[...] = acc[0:8, :] + acc[1:2, :]


def gain_query(info, base, pieces, gain, weight):
    return pl.pallas_call(
        functools.partial(gain_body, base, pieces),
        out_shape=jax.ShapeDtypeStruct((8, weight.shape[1]), jnp.float32),
        in_specs=[pl.BlockSpec(memory_space=pltpu.SMEM)] + [pl.BlockSpec(memory_space=pltpu.VMEM)] * 2,
        out_specs=pl.BlockSpec(memory_space=pltpu.VMEM),
        compiler_params=pltpu.CompilerParams(vmem_limit_bytes=CROSS_VMEM),
        name="gain",
    )(info, gain, weight)


def early_body(base, which, info, *refs):
    count = len(which)
    parts, (gain, weight, out, stat) = refs[:count], refs[count:]
    total, squares = row_sums(parts)
    center = total / (count * parts[0].shape[1])
    out[...] = centred(info, base, which, parts, center, gain, weight)
    lane = lax.broadcasted_iota(jnp.int32, stat.shape, 1)
    stat[...] = jnp.where(lane == 0, center, jnp.where(lane == 1, total, squares))


def early_query(info, base, which, parts, gain, weight):
    rows = parts[0].shape[0]
    operands = [*parts, gain, weight]
    return pl.pallas_call(
        functools.partial(early_body, base, which),
        out_shape=[
            jax.ShapeDtypeStruct((rows, weight.shape[1]), jnp.float32),
            jax.ShapeDtypeStruct((rows, 128), jnp.float32),
        ],
        in_specs=[pl.BlockSpec(memory_space=pltpu.SMEM)]
        + [pl.BlockSpec(memory_space=pltpu.VMEM)] * len(operands),
        out_specs=[pl.BlockSpec(memory_space=pltpu.VMEM)] * 2,
        compiler_params=pltpu.CompilerParams(vmem_limit_bytes=CROSS_VMEM),
        name="early",
    )(info, *operands)


def normed_query(info, base, which, refs):
    parts, (gain, weight, early, stat, gained) = refs[: len(which)], refs[len(which) :]
    center = stat[:, 0:1]
    total, squares = row_sums(parts)
    mean = (stat[:, 1:2] + total) / D
    scale = lax.rsqrt((stat[:, 2:3] + squares) / D - mean * mean + 1e-06)
    acc = early[...] + centred(info, base, which, parts, center, gain, weight)
    return (scale * (acc - (mean - center) * gained[0:1, :])).astype(jnp.bfloat16)


def answer(query, texts, length, block):
    width = block.shape[1]
    for h in range(width // HD):
        cols = slice(h * HD, (h + 1) * HD)
        total = 0.0
        mixed = 0.0
        first = 0
        for text in texts:
            token = first + lax.broadcasted_iota(jnp.int32, (1, text.shape[0]), 1)
            first += text.shape[0]
            scores = dot(query[:, cols], text[:, cols], ((1,), (1,))) * FACTOR
            weights = jnp.exp(jnp.where(token < length, scores, -1e30))
            total = total + jnp.sum(weights, axis=1, keepdims=True)
            values = text[:, width + h * HD : width + (h + 1) * HD]
            mixed = mixed + dot(weights.astype(jnp.bfloat16), values, ((1,), (0,)))
        block[:, cols] = (mixed / total).astype(jnp.bfloat16)


def query_body(which, base, info, *refs):
    refs[-1][...] = normed_query(info, base, which, refs[:-1])


def cross_body(which, sources, count, base, limit, start, info, *refs):
    texts, refs = refs[:count], refs[count:]
    out, block, sem = refs[-3:]
    query = normed_query(info, base, which, refs[:sources]) if sources > 1 else refs[0][...]
    answer(query, texts, info[limit], block)
    copy = pltpu.make_async_copy(block, out.at[pl.ds(start, block.shape[0]), :], sem)
    copy.start()
    copy.wait()


def cross_query(info, base, which, sources, width):
    in_specs = [pl.BlockSpec(memory_space=pltpu.SMEM)]
    return pl.pallas_call(
        functools.partial(query_body, which, base),
        out_shape=jax.ShapeDtypeStruct((sources[0].shape[0], width), jnp.bfloat16),
        in_specs=in_specs + [pl.BlockSpec(memory_space=pltpu.VMEM)] * len(sources),
        out_specs=pl.BlockSpec(memory_space=pltpu.VMEM),
        compiler_params=pltpu.CompilerParams(vmem_limit_bytes=CROSS_VMEM),
        name="query",
    )(info, *sources)


def cross(info, base, limit, texts, which, sources, width, start, total_rows, done):
    rows = sources[0].shape[0]
    operands = [info, *texts, *sources]
    in_specs = [pl.BlockSpec(memory_space=pltpu.SMEM)]
    in_specs += [pl.BlockSpec(memory_space=pltpu.VMEM)] * (len(operands) - 1)
    aliases = {}
    if done is not None:
        aliases = {len(operands): 0}
        operands.append(done)
        in_specs.append(pl.BlockSpec(memory_space=pl.ANY))
    return pl.pallas_call(
        functools.partial(cross_body, which, len(sources), len(texts), base, limit, start),
        out_shape=jax.ShapeDtypeStruct((total_rows, width), jnp.bfloat16),
        in_specs=in_specs,
        out_specs=pl.BlockSpec(memory_space=pl.ANY),
        scratch_shapes=[pltpu.VMEM((rows, width), jnp.bfloat16), pltpu.SemaphoreType.DMA(())],
        input_output_aliases=aliases,
        compiler_params=pltpu.CompilerParams(vmem_limit_bytes=CROSS_VMEM),
        name="cross",
    )(*operands)


def unpack_wide(x, width):
    return jnp.concatenate([x[:, n : n + width] for n in range(0, x.shape[1], width)])


def wide_unpack(x, count):
    return jnp.concatenate([x[n : n + count] for n in range(0, x.shape[0], count)], axis=1)


def after(value, *others):
    return lax.optimization_barrier((value, others))[0]


def self_line(info, left_check, query, key, value, heads, seq_size, right, left):
    same = lambda g: g
    pair = lambda k, v, check: ((k, same), (v, same), check)
    from_left = from_right = (key, value)
    state = attend(info, (query, same), [pair(key, value, None)], None, seq_size == 1, 1, heads)
    for step in range(1, seq_size):
        from_left = tuple(right(x) for x in from_left)
        from_right = tuple(left(x) for x in from_right)
        blocks = [
            pair(*from_left, left_check + 2 * (step - 1)),
            pair(*from_right, left_check + 2 * (step - 1) + 1),
        ]
        state = attend(info, (query, same), blocks, state, step == seq_size - 1, 1, heads)
    return state[0]


def text_line(text_part, square_part, place, seq_size, right, left):
    share = text_part.shape[0] // seq_size

    def rows_of(array, owner):
        return lax.dynamic_slice_in_dim(array, jnp.clip(owner, 0, seq_size - 1) * share, share)

    rightward = leftward = None
    for step in range(1, seq_size):
        ahead, behind = place + seq_size - step, place - seq_size + step
        to_right = rows_of(text_part, ahead), rows_of(square_part, ahead)
        to_left = rows_of(text_part, behind), rows_of(square_part, behind)
        if step > 1:
            to_right = tuple(a + b.astype(jnp.float32) for a, b in zip(to_right, rightward))
            to_left = tuple(a + b.astype(jnp.float32) for a, b in zip(to_left, leftward))
        rightward = right(to_right[0].astype(jnp.bfloat16), step), right(to_right[1], step)
        leftward = left(to_left[0].astype(jnp.bfloat16), step), left(to_left[1], step)
    text_sum, square_sum = (
        rows_of(own, place) + a.astype(jnp.float32) + b.astype(jnp.float32)
        for own, a, b in zip((text_part, square_part), rightward, leftward)
    )
    text_low = (text_sum / jnp.sqrt(square_sum / DT + 1e-06)[:, None]).astype(jnp.bfloat16)
    return lax.all_gather(text_low, "seq", axis=0, tiled=True)


def shards(
    seq_size,
    tensor_size,
    video_states,
    query_self,
    key_self,
    value_self,
    out_weight,
    cross_gain,
    query_weight,
    text_memory,
    text_gain,
    text_weight,
    prompt_length,
):
    local_rows, local_width = query_self.shape
    heads = local_width // HD
    place = lax.axis_index("seq")
    slot = lax.axis_index("tensor")
    paired = tensor_size == 4
    four = seq_size == 4 and heads == 6 and text_memory.shape[0] * 3 == local_rows * 4
    piece = cross_gain.shape[0]

    def right(x, most=seq_size):
        return lax.ppermute(x, "seq", [(n, n + 1) for n in range(min(most, seq_size - 1))])

    def left(x, most=seq_size):
        last = seq_size - 1
        return lax.ppermute(x, "seq", [(last - n, last - n - 1) for n in range(min(most, last))])

    def swap(x, bit):
        return lax.ppermute(x, "tensor", [(n, n ^ bit) for n in range(tensor_size)])

    is_end = (place == 0) | (place == seq_size - 1)
    if paired:
        order = [slot ^ 1, slot ^ 3, slot, slot ^ 2, slot ^ 1, slot ^ 3]
    else:
        order = [jnp.int32(n) for n in range(tensor_size)]
    scalars = [prompt_length[0], is_end, ~is_end] + order
    line_check = len(scalars)
    for step in range(1, seq_size):
        scalars += [place >= step, place + step < seq_size]
    info = jnp.stack([jnp.asarray(s).astype(jnp.int32) for s in scalars])
    LIMIT, END, MIDDLE, ORDER = 0, 1, 2, 3

    def text_parts(memory, gain, weight):
        memory_float = memory.astype(jnp.float32)
        scaled_text = (memory_float * gain).astype(jnp.bfloat16)
        square_part = jnp.sum(memory_float * memory_float, axis=1)
        text_part = jnp.dot(
            scaled_text, weight.reshape(weight.shape[0], -1), preferred_element_type=jnp.float32
        )
        return text_part, square_part

    if local_rows % 384 == 0:
        chunks = [(0, local_rows * 2 // 3), (local_rows * 2 // 3, local_rows // 3)]
    else:
        chunks = [(0, local_rows)]
    if four:
        def outer(x):
            return lax.ppermute(x, "seq", [(0, 1), (1, 0), (2, 3), (3, 2)])

        def inner(x):
            return lax.ppermute(x, "seq", [(0, 0), (1, 2), (2, 1), (3, 3)])

        cut = 2 * HD
        kept = lambda k, v, base, check: ((k, lambda g: g + base), (v, lambda g: g + base), check)
        lend = lambda k, v, check: ((k, lambda g: 0), (v, lambda g: 0), check)
        query_kept = (query_self, lambda g: g + 1)

        def fold(query, blocks, state, last=False):
            return attend(info, query, blocks, state, last, 2, 2)

        inner_1v, inner_1k = inner(value_self), inner(key_self)
        kept_k, kept_v = trim(key_self, value_self, cut)
        outer_1v, outer_1k = outer(kept_v), outer(kept_k)
        state = fold(query_kept, [kept(key_self, value_self, 1, None)], None)
        (text_memory, text_gain, text_weight, cross_gain), state = lax.optimization_barrier(
            ((text_memory, text_gain, text_weight, cross_gain), state)
        )
        query_lent = query_self[:, :cut]
        text_part, square_part = text_parts(text_memory, text_gain, text_weight)
        text_low = text_part.astype(jnp.bfloat16)
        rows = text_part.shape[0]
        eighth = rows // 8

        def pack(start, stop):
            x = text_low[start * eighth : stop * eighth]
            width = x.shape[0] * x.shape[1] // local_rows
            return jnp.concatenate([x[:, n : n + width] for n in range(0, x.shape[1], width)])

        def unpack(x, count):
            count = count * eighth
            return jnp.concatenate([x[n : n + count] for n in range(0, x.shape[0], count)], axis=1)

        inner_2v = inner(outer_1v)
        given = jnp.where(is_end, jnp.concatenate([key_self[:, :cut], value_self[:, :cut]], axis=1), inner_1v[:, cut:])
        outer_2v = outer(given)
        inner_2k = inner(outer_1k)
        query_pack = jnp.concatenate([query_lent, pack(0, 1)], axis=1)
        given = jnp.where(is_end, query_pack, inner_1k[:, cut:])
        outer_2k = outer(given)
        square_sum = square_part + outer(square_part)
        state = fold(query_kept, [kept(outer_1k, outer_1v, 0, None), kept(inner_1k, inner_1v, 1, MIDDLE)], state)
        inner_2a = inner(outer_2v)
        outer_3v = outer(jnp.where(is_end, pack(1, 3), inner_2v))
        both_lent = (jnp.concatenate([query_lent, outer_2k[:, :cut]], axis=1), lambda g: g)
        near = ((outer_2v, lambda g: 0), (outer_2v, lambda g: 1), MIDDLE)
        far = ((inner_2a, lambda g: 0), (inner_2a, lambda g: 1), MIDDLE)
        loan = fold(both_lent, [lend(key_self, value_self, None), near, lend(inner_1k, inner_1v, MIDDLE)], None)
        outer_3k = outer(jnp.where(is_end, pack(3, 5), inner_2k))
        loan = fold(both_lent, [far], loan, True)[0]
        given = jnp.where(
            is_end, unpack_wide(text_low[5 * eighth : 6 * eighth], loan.shape[1]), loan[cut:]
        )
        back = outer(given)
        text_sums, text_others, start = [], [], 0

        def add_text(*parts):
            rows = sum(part.shape[0] for part in parts)
            part = jnp.concatenate(parts) if len(parts) > 1 else parts[0]
            part = after(part, *text_sums)
            own = lax.optimization_barrier(text_part[start : start + rows] + part.astype(jnp.float32))
            text_sums.append(own)
            text_others.append(inner(own.astype(jnp.bfloat16)))
            return start + rows

        start = add_text(unpack(outer_2k[:, cut:], 1), unpack(outer_3v, 2))
        root = jnp.sqrt((square_sum + inner(square_sum)) / DT + 1e-06)
        state = fold(query_kept, [kept(outer_2k, outer_2v, 0, END), kept(inner_2k, inner_2v, 0, MIDDLE)], state)
        rest = fold(query_kept, [kept(outer_3k, outer_3v, 0, END)], state, True)[0]
        mixed = [loan[:cut], back, rest]
        mixed_check = END
    else:
        mixed = [self_line(info, line_check, query_self, key_self, value_self, heads, seq_size, right, left)]
        mixed_check = None
        text_part, square_part = text_parts(text_memory, text_gain, text_weight)
        texts = [text_line(text_part, square_part, place, seq_size, right, left)]

    if paired:
        gain_two = jnp.stack([cross_gain, swap(cross_gain, 2)])
        gain_all = jnp.concatenate([gain_two, swap(gain_two, 1)]).reshape(1, -1)
        overs, mines, sents = [], [], []
        for start_row, rows in chunks:
            spot = (mixed_check, start_row, rows, out_weight, tensor_size)
            theirs = project(info, mixed, *spot, ORDER, 2)
            sent = after(swap(theirs, 1), *overs)
            own = project(info, mixed, *spot, ORDER + 2, 2)
            total = own[:, piece:].astype(jnp.float32) + sent[:, piece:].astype(jnp.float32)
            overs.append(total.astype(jnp.bfloat16))
            mines.append(own)
            sents.append(sent)
        others = [swap(x, 2) for x in overs]
    else:
        gain_all = lax.all_gather(cross_gain, "tensor", axis=0, tiled=True).reshape(1, -1)
        partials = [
            project(info, mixed, mixed_check, start_row, rows, out_weight, tensor_size, ORDER, tensor_size)
            for start_row, rows in chunks
        ]
    if four:
        start = add_text(unpack(outer_3k, 2), wide_unpack(back, eighth))
        texts, row = [], 0
        for n in range(3):
            own, other = text_sums[n], text_others[n]
            share = root[row : row + own.shape[0]]
            row += own.shape[0]
            total = ((own + other.astype(jnp.float32)) / share[:, None]).astype(jnp.bfloat16)
            given = jnp.where(is_end, text_low[5 * eighth :], total) if n == 0 else total
            taken = outer(given)
            texts.append(jnp.where(is_end, taken, total))
            if n == 0:
                add_text(taken[eighth:])
    out, residuals = None, []
    for n, (start_row, rows) in enumerate(chunks):
        video = video_states[start_row : start_row + rows].astype(jnp.float32)
        if paired:
            residual = (
                video
                + mines[n][:, :piece].astype(jnp.float32)
                + sents[n][:, :piece].astype(jnp.float32)
                + after(others[n], *residuals).astype(jnp.float32)
            ).astype(jnp.bfloat16)
            across = swap(residual, 2)
            parts = [residual, across, swap(residual, 1), swap(across, 1)]
            base = ORDER + 2
        else:
            summed = lax.psum_scatter(partials[n], "tensor", scatter_dimension=1, tiled=True)
            residual = (video + summed.astype(jnp.float32)).astype(jnp.bfloat16)
            gathered = lax.all_gather(residual, "tensor", axis=1, tiled=True)
            parts = [gathered[:, m * piece : (m + 1) * piece] for m in range(tensor_size)]
            base = ORDER
        residuals.append(residual)
        soon = [m for m in range(tensor_size) if m % 2 == 0]
        later = [m for m in range(tensor_size) if m % 2 == 1]
        if n == 0:
            gained = gain_query(info, base, tensor_size, gain_all, query_weight)
        first = early_query(info, base, soon, [parts[m] for m in soon], gain_all, query_weight)
        sources = [*(parts[m] for m in later), gain_all, query_weight, *first, gained]
        if n < len(chunks) - 1:
            sources = [cross_query(info, base, later, sources, local_width)]
        spot = (local_width, start_row, local_rows, out)
        out = cross(info, base, LIMIT, texts, later, sources, *spot)
    return (jnp.concatenate(residuals), out)


def solution(mesh):
    in_specs = (
        P(("groups", "seq"), "tensor"),
        P(("groups", "seq"), "tensor"),
        P(("groups", "seq"), "tensor"),
        P(("groups", "seq"), "tensor"),
        P("tensor", None),
        P("tensor"),
        P(None, "tensor"),
        P("groups", "seq"),
        P("seq"),
        P("seq", None, "tensor"),
        P("groups"),
    )
    out_specs = (P(("groups", "seq"), "tensor"), P(("groups", "seq"), "tensor"))

    def body(*args):
        return shards(mesh.shape["seq"], mesh.shape["tensor"], *args)

    return jax.shard_map(body, mesh=mesh, in_specs=in_specs, out_specs=out_specs, check_vma=False)
```

```python
import functools
import math

import jax
import jax.numpy as jnp
from jax import lax
from jax.experimental import pallas as pl
from jax.experimental.pallas import tpu as pltpu
from jax.sharding import PartitionSpec as P


D = 5120
DT = 4096
HD = 128
FACTOR = 1.0 / math.sqrt(HD)
EXP2 = FACTOR * math.log2(math.e)

ATTEND_VMEM = 16 << 20
PROJECT_VMEM = 24 << 20
CROSS_VMEM = 28 << 20


def dot(a, b, dims):
    return lax.dot_general(a, b, (dims, ((), ())), preferred_element_type=jnp.float32)


def attend_body(per, checks, first, last, info, query, *refs):
    count = len(checks)
    blocks = refs[: 2 * count]
    refs = refs[2 * count :]
    if not first:
        stat_in, acc_in = refs[:2]
        refs = refs[2:]
    outs, (stat, acc) = refs[:-2], refs[-2:]
    if not first:
        stat[...] = stat_in[...]
        acc[...] = acc_in[...]
    for n, check in enumerate(checks):
        key, value = blocks[2 * n], blocks[2 * n + 1]
        fresh = first and n == 0

        def fold(key=key, value=value, fresh=fresh):
            for h in range(per):
                cols = slice(h * HD, (h + 1) * HD)
                top_row, sum_row = slice(8 * h, 8 * h + 1), slice(8 * h + 1, 8 * h + 2)
                scores = dot(key[:, cols], query[:, cols], ((1,), (1,)))
                top = jnp.max(scores, axis=0, keepdims=True)
                if not fresh:
                    old = stat[top_row, :]
                    top = jnp.maximum(old, top)
                weights = jnp.exp2((scores - top) * EXP2)
                total = jnp.sum(weights, axis=0, keepdims=True)
                mixed = dot(value[:, cols], weights.astype(jnp.bfloat16), ((0,), (0,)))
                if not fresh:
                    shrink = jnp.exp2((old - top) * EXP2)
                    total = total + stat[sum_row, :] * shrink
                    mixed = mixed + acc[cols, :] * shrink
                stat[top_row, :] = top
                stat[sum_row, :] = total
                acc[cols, :] = mixed

        if check is None:
            fold()
        else:
            pl.when(info[check] > 0)(fold)
    if last:
        for h in range(per):
            cols = slice(h * HD, (h + 1) * HD)
            outs[0][cols, :] = (acc[cols, :] / stat[8 * h + 1 : 8 * h + 2, :]).astype(jnp.bfloat16)
    else:
        outs[0][...] = stat[...]
        outs[1][...] = acc[...]


def attend(info, query, blocks, state, last, per, groups):
    rows = query[0].shape[0]
    first = state is None

    def spec(pair):
        array, index = pair
        return pl.BlockSpec((array.shape[0], per * HD), lambda g, i: (0, index(g)))

    in_specs = [spec(query)]
    operands = [query[0]]
    for key, value, check in blocks:
        in_specs += [spec(key), spec(value)]
        operands += [key[0], value[0]]
    stat_spec = pl.BlockSpec((8 * per, rows), lambda g, i: (g, 0))
    acc_spec = pl.BlockSpec((HD * per, rows), lambda g, i: (g, 0))
    if not first:
        in_specs += [stat_spec, acc_spec]
        operands += list(state)
    width = HD * per * groups
    if last:
        out_shape = [jax.ShapeDtypeStruct((width, rows), jnp.bfloat16)]
        out_specs = [acc_spec]
    else:
        out_shape = [
            jax.ShapeDtypeStruct((8 * per * groups, rows), jnp.float32),
            jax.ShapeDtypeStruct((width, rows), jnp.float32),
        ]
        out_specs = [stat_spec, acc_spec]
    return pl.pallas_call(
        functools.partial(attend_body, per, [b[2] for b in blocks], first, last),
        out_shape=out_shape,
        grid_spec=pltpu.PrefetchScalarGridSpec(
            num_scalar_prefetch=1,
            grid=(groups,),
            in_specs=in_specs,
            out_specs=out_specs,
            scratch_shapes=[
                pltpu.VMEM((8 * per, rows), jnp.float32),
                pltpu.VMEM((HD * per, rows), jnp.float32),
            ],
        ),
        compiler_params=pltpu.CompilerParams(vmem_limit_bytes=ATTEND_VMEM),
        name="attend",
    )(info, *operands)


def trim_body(cut, key, value, key_kept, value_kept, sems):
    rest = pl.ds(cut, key_kept.shape[1])
    pairs = [
        (value.at[:, rest], value_kept),
        (key.at[:, rest], key_kept),
    ]
    copies = [pltpu.make_async_copy(*pair, sems.at[n]) for n, pair in enumerate(pairs)]
    for copy in copies:
        copy.start()
    for copy in copies:
        copy.wait()


def trim(key, value, cut):
    rows, width = key.shape
    kept = jax.ShapeDtypeStruct((rows, width - cut), key.dtype)
    return pl.pallas_call(
        functools.partial(trim_body, cut),
        out_shape=[kept, kept],
        in_specs=[pl.BlockSpec(memory_space=pl.ANY)] * 2,
        out_specs=[pl.BlockSpec(memory_space=pl.ANY)] * 2,
        scratch_shapes=[pltpu.SemaphoreType.DMA((2,))],
        compiler_params=pltpu.CompilerParams(vmem_limit_bytes=ATTEND_VMEM),
        name="trim",
    )(key, value)


def project_body(check, info, *refs):
    mixed, weight, out = refs[:-2], refs[-2], refs[-1]
    if check is None:
        total = dot(mixed[0][...], weight[...], ((0,), (0,)))
    else:
        near, far, rest = mixed
        lead = jnp.where(info[check] > 0, far[...], near[...])
        cut = lead.shape[0]
        total = dot(lead, weight[:cut, :], ((0,), (0,))) + dot(rest[...], weight[cut:, :], ((0,), (0,)))
    out[...] = total.astype(jnp.bfloat16)


def project(info, mixed, check, start, rows, weight, pieces, base, count):
    piece = weight.shape[1] // pieces
    return pl.pallas_call(
        functools.partial(project_body, check),
        out_shape=jax.ShapeDtypeStruct((rows, piece * count), jnp.bfloat16),
        grid_spec=pltpu.PrefetchScalarGridSpec(
            num_scalar_prefetch=1,
            grid=(count,),
            in_specs=[pl.BlockSpec((m.shape[0], rows), lambda p, i: (0, start // rows)) for m in mixed]
            + [pl.BlockSpec((weight.shape[0], piece), lambda p, i: (0, i[base + p]))],
            out_specs=pl.BlockSpec((rows, piece), lambda p, i: (0, p)),
        ),
        compiler_params=pltpu.CompilerParams(vmem_limit_bytes=PROJECT_VMEM),
        name="project",
    )(info, *mixed, weight)


def centred(info, base, which, parts, center, gain, weight):
    piece = parts[0].shape[1]
    acc = 0.0
    for n, part in zip(which, parts):
        value = part[...].astype(jnp.float32)
        value = ((value - center) * gain[:, n * piece : (n + 1) * piece]).astype(jnp.bfloat16)
        spot = pl.ds(pl.multiple_of(info[base + n] * piece, piece), piece)
        acc = acc + dot(value, weight[spot, :], ((1,), (0,)))
    return acc


def row_sums(parts):
    total = squares = 0.0
    for part in parts:
        value = part[...].astype(jnp.float32)
        total = total + jnp.sum(value, axis=1, keepdims=True)
        squares = squares + jnp.sum(value * value, axis=1, keepdims=True)
    return total, squares


def gain_body(base, pieces, info, gain, weight, out):
    piece = gain.shape[1] // pieces
    row = lax.broadcasted_iota(jnp.int32, (16, piece), 0)
    acc = 0.0
    for n in range(pieces):
        whole = gain[:, n * piece : (n + 1) * piece]
        high = whole.astype(jnp.bfloat16).astype(jnp.float32)
        both = jnp.where(row == 0, high, jnp.where(row == 1, whole - high, 0.0)).astype(jnp.bfloat16)
        spot = pl.ds(pl.multiple_of(info[base + n] * piece, piece), piece)
        acc = acc + dot(both, weight[spot, :], ((1,), (0,)))
    out[...] = acc[0:8, :] + acc[1:2, :]


def gain_query(info, base, pieces, gain, weight):
    return pl.pallas_call(
        functools.partial(gain_body, base, pieces),
        out_shape=jax.ShapeDtypeStruct((8, weight.shape[1]), jnp.float32),
        in_specs=[pl.BlockSpec(memory_space=pltpu.SMEM)] + [pl.BlockSpec(memory_space=pltpu.VMEM)] * 2,
        out_specs=pl.BlockSpec(memory_space=pltpu.VMEM),
        compiler_params=pltpu.CompilerParams(vmem_limit_bytes=CROSS_VMEM),
        name="gain",
    )(info, gain, weight)


def early_body(base, which, info, *refs):
    count = len(which)
    parts, (gain, weight, out, stat) = refs[:count], refs[count:]
    total, squares = row_sums(parts)
    center = total / (count * parts[0].shape[1])
    out[...] = centred(info, base, which, parts, center, gain, weight)
    lane = lax.broadcasted_iota(jnp.int32, stat.shape, 1)
    stat[...] = jnp.where(lane == 0, center, jnp.where(lane == 1, total, squares))


def early_query(info, base, which, parts, gain, weight):
    rows = parts[0].shape[0]
    operands = [*parts, gain, weight]
    return pl.pallas_call(
        functools.partial(early_body, base, which),
        out_shape=[
            jax.ShapeDtypeStruct((rows, weight.shape[1]), jnp.float32),
            jax.ShapeDtypeStruct((rows, 128), jnp.float32),
        ],
        in_specs=[pl.BlockSpec(memory_space=pltpu.SMEM)]
        + [pl.BlockSpec(memory_space=pltpu.VMEM)] * len(operands),
        out_specs=[pl.BlockSpec(memory_space=pltpu.VMEM)] * 2,
        compiler_params=pltpu.CompilerParams(vmem_limit_bytes=CROSS_VMEM),
        name="early",
    )(info, *operands)


def normed_query(info, base, which, refs):
    parts, (gain, weight, early, stat, gained) = refs[: len(which)], refs[len(which) :]
    center = stat[:, 0:1]
    total, squares = row_sums(parts)
    mean = (stat[:, 1:2] + total) / D
    scale = lax.rsqrt((stat[:, 2:3] + squares) / D - mean * mean + 1e-06)
    acc = early[...] + centred(info, base, which, parts, center, gain, weight)
    return (scale * (acc - (mean - center) * gained[0:1, :])).astype(jnp.bfloat16)


def answer(query, texts, length, block):
    width = block.shape[1]
    for h in range(width // HD):
        cols = slice(h * HD, (h + 1) * HD)
        total = 0.0
        mixed = 0.0
        first = 0
        for text in texts:
            token = first + lax.broadcasted_iota(jnp.int32, (1, text.shape[0]), 1)
            first += text.shape[0]
            scores = dot(query[:, cols], text[:, cols], ((1,), (1,))) * FACTOR
            weights = jnp.exp(jnp.where(token < length, scores, -1e30))
            total = total + jnp.sum(weights, axis=1, keepdims=True)
            values = text[:, width + h * HD : width + (h + 1) * HD]
            mixed = mixed + dot(weights.astype(jnp.bfloat16), values, ((1,), (0,)))
        block[:, cols] = (mixed / total).astype(jnp.bfloat16)


def query_body(which, base, info, *refs):
    refs[-1][...] = normed_query(info, base, which, refs[:-1])


def cross_body(which, sources, count, base, limit, start, info, *refs):
    texts, refs = refs[:count], refs[count:]
    out, block, sem = refs[-3:]
    query = normed_query(info, base, which, refs[:sources]) if sources > 1 else refs[0][...]
    answer(query, texts, info[limit], block)
    copy = pltpu.make_async_copy(block, out.at[pl.ds(start, block.shape[0]), :], sem)
    copy.start()
    copy.wait()


def cross_query(info, base, which, sources, width):
    in_specs = [pl.BlockSpec(memory_space=pltpu.SMEM)]
    return pl.pallas_call(
        functools.partial(query_body, which, base),
        out_shape=jax.ShapeDtypeStruct((sources[0].shape[0], width), jnp.bfloat16),
        in_specs=in_specs + [pl.BlockSpec(memory_space=pltpu.VMEM)] * len(sources),
        out_specs=pl.BlockSpec(memory_space=pltpu.VMEM),
        compiler_params=pltpu.CompilerParams(vmem_limit_bytes=CROSS_VMEM),
        name="query",
    )(info, *sources)


def cross(info, base, limit, texts, which, sources, width, start, total_rows, done):
    rows = sources[0].shape[0]
    operands = [info, *texts, *sources]
    in_specs = [pl.BlockSpec(memory_space=pltpu.SMEM)]
    in_specs += [pl.BlockSpec(memory_space=pltpu.VMEM)] * (len(operands) - 1)
    aliases = {}
    if done is not None:
        aliases = {len(operands): 0}
        operands.append(done)
        in_specs.append(pl.BlockSpec(memory_space=pl.ANY))
    return pl.pallas_call(
        functools.partial(cross_body, which, len(sources), len(texts), base, limit, start),
        out_shape=jax.ShapeDtypeStruct((total_rows, width), jnp.bfloat16),
        in_specs=in_specs,
        out_specs=pl.BlockSpec(memory_space=pl.ANY),
        scratch_shapes=[pltpu.VMEM((rows, width), jnp.bfloat16), pltpu.SemaphoreType.DMA(())],
        input_output_aliases=aliases,
        compiler_params=pltpu.CompilerParams(vmem_limit_bytes=CROSS_VMEM),
        name="cross",
    )(*operands)


def unpack_wide(x, width):
    return jnp.concatenate([x[:, n : n + width] for n in range(0, x.shape[1], width)])


def wide_unpack(x, count):
    return jnp.concatenate([x[n : n + count] for n in range(0, x.shape[0], count)], axis=1)


def after(value, *others):
    return lax.optimization_barrier((value, others))[0]


def self_line(info, left_check, query, key, value, heads, seq_size, right, left):
    same = lambda g: g
    pair = lambda k, v, check: ((k, same), (v, same), check)
    from_left = from_right = (key, value)
    state = attend(info, (query, same), [pair(key, value, None)], None, seq_size == 1, 1, heads)
    for step in range(1, seq_size):
        from_left = tuple(right(x) for x in from_left)
        from_right = tuple(left(x) for x in from_right)
        blocks = [
            pair(*from_left, left_check + 2 * (step - 1)),
            pair(*from_right, left_check + 2 * (step - 1) + 1),
        ]
        state = attend(info, (query, same), blocks, state, step == seq_size - 1, 1, heads)
    return state[0]


def text_line(text_part, square_part, place, seq_size, right, left):
    share = text_part.shape[0] // seq_size

    def rows_of(array, owner):
        return lax.dynamic_slice_in_dim(array, jnp.clip(owner, 0, seq_size - 1) * share, share)

    rightward = leftward = None
    for step in range(1, seq_size):
        ahead, behind = place + seq_size - step, place - seq_size + step
        to_right = rows_of(text_part, ahead), rows_of(square_part, ahead)
        to_left = rows_of(text_part, behind), rows_of(square_part, behind)
        if step > 1:
            to_right = tuple(a + b.astype(jnp.float32) for a, b in zip(to_right, rightward))
            to_left = tuple(a + b.astype(jnp.float32) for a, b in zip(to_left, leftward))
        rightward = right(to_right[0].astype(jnp.bfloat16), step), right(to_right[1], step)
        leftward = left(to_left[0].astype(jnp.bfloat16), step), left(to_left[1], step)
    text_sum, square_sum = (
        rows_of(own, place) + a.astype(jnp.float32) + b.astype(jnp.float32)
        for own, a, b in zip((text_part, square_part), rightward, leftward)
    )
    text_low = (text_sum / jnp.sqrt(square_sum / DT + 1e-06)[:, None]).astype(jnp.bfloat16)
    return lax.all_gather(text_low, "seq", axis=0, tiled=True)


def shards(
    seq_size,
    tensor_size,
    video_states,
    query_self,
    key_self,
    value_self,
    out_weight,
    cross_gain,
    query_weight,
    text_memory,
    text_gain,
    text_weight,
    prompt_length,
):
    local_rows, local_width = query_self.shape
    heads = local_width // HD
    place = lax.axis_index("seq")
    slot = lax.axis_index("tensor")
    paired = tensor_size == 4
    four = seq_size == 4 and heads == 6 and text_memory.shape[0] * 3 == local_rows * 4
    piece = cross_gain.shape[0]

    def right(x, most=seq_size):
        return lax.ppermute(x, "seq", [(n, n + 1) for n in range(min(most, seq_size - 1))])

    def left(x, most=seq_size):
        last = seq_size - 1
        return lax.ppermute(x, "seq", [(last - n, last - n - 1) for n in range(min(most, last))])

    def swap(x, bit):
        return lax.ppermute(x, "tensor", [(n, n ^ bit) for n in range(tensor_size)])

    is_end = (place == 0) | (place == seq_size - 1)
    if paired:
        order = [slot ^ 1, slot ^ 3, slot, slot ^ 2, slot ^ 1, slot ^ 3]
    else:
        order = [jnp.int32(n) for n in range(tensor_size)]
    scalars = [prompt_length[0], is_end, ~is_end] + order
    line_check = len(scalars)
    for step in range(1, seq_size):
        scalars += [place >= step, place + step < seq_size]
    info = jnp.stack([jnp.asarray(s).astype(jnp.int32) for s in scalars])
    LIMIT, END, MIDDLE, ORDER = 0, 1, 2, 3

    def text_parts(memory, gain, weight):
        memory_float = memory.astype(jnp.float32)
        scaled_text = (memory_float * gain).astype(jnp.bfloat16)
        square_part = jnp.sum(memory_float * memory_float, axis=1)
        text_part = jnp.dot(
            scaled_text, weight.reshape(weight.shape[0], -1), preferred_element_type=jnp.float32
        )
        return text_part, square_part

    if local_rows % 384 == 0:
        chunks = [(0, local_rows * 2 // 3), (local_rows * 2 // 3, local_rows // 3)]
    else:
        chunks = [(0, local_rows)]
    if four:
        def outer(x):
            return lax.ppermute(x, "seq", [(0, 1), (1, 0), (2, 3), (3, 2)])

        def inner(x):
            return lax.ppermute(x, "seq", [(0, 0), (1, 2), (2, 1), (3, 3)])

        cut = 2 * HD
        kept = lambda k, v, base, check: ((k, lambda g: g + base), (v, lambda g: g + base), check)
        lend = lambda k, v, check: ((k, lambda g: 0), (v, lambda g: 0), check)
        query_kept = (query_self, lambda g: g + 1)

        def fold(query, blocks, state, last=False):
            return attend(info, query, blocks, state, last, 2, 2)

        inner_1v, inner_1k = inner(value_self), inner(key_self)
        kept_k, kept_v = trim(key_self, value_self, cut)
        outer_1v, outer_1k = outer(kept_v), outer(kept_k)
        state = fold(query_kept, [kept(key_self, value_self, 1, None)], None)
        (text_memory, text_gain, text_weight, cross_gain), state = lax.optimization_barrier(
            ((text_memory, text_gain, text_weight, cross_gain), state)
        )
        query_lent = query_self[:, :cut]
        text_part, square_part = text_parts(text_memory, text_gain, text_weight)
        text_low = text_part.astype(jnp.bfloat16)
        rows = text_part.shape[0]
        eighth = rows // 8

        def pack(start, stop):
            x = text_low[start * eighth : stop * eighth]
            width = x.shape[0] * x.shape[1] // local_rows
            return jnp.concatenate([x[:, n : n + width] for n in range(0, x.shape[1], width)])

        def unpack(x, count):
            count = count * eighth
            return jnp.concatenate([x[n : n + count] for n in range(0, x.shape[0], count)], axis=1)

        inner_2v = inner(outer_1v)
        given = jnp.where(is_end, jnp.concatenate([key_self[:, :cut], value_self[:, :cut]], axis=1), inner_1v[:, cut:])
        outer_2v = outer(given)
        inner_2k = inner(outer_1k)
        query_pack = jnp.concatenate([query_lent, pack(0, 1)], axis=1)
        given = jnp.where(is_end, query_pack, inner_1k[:, cut:])
        outer_2k = outer(given)
        square_sum = square_part + outer(square_part)
        state = fold(query_kept, [kept(outer_1k, outer_1v, 0, None), kept(inner_1k, inner_1v, 1, MIDDLE)], state)
        inner_2a = inner(outer_2v)
        outer_3v = outer(jnp.where(is_end, pack(1, 3), inner_2v))
        both_lent = (jnp.concatenate([query_lent, outer_2k[:, :cut]], axis=1), lambda g: g)
        near = ((outer_2v, lambda g: 0), (outer_2v, lambda g: 1), MIDDLE)
        far = ((inner_2a, lambda g: 0), (inner_2a, lambda g: 1), MIDDLE)
        loan = fold(both_lent, [lend(key_self, value_self, None), near, lend(inner_1k, inner_1v, MIDDLE)], None)
        outer_3k = outer(jnp.where(is_end, pack(3, 5), inner_2k))
        loan = fold(both_lent, [far], loan, True)[0]
        given = jnp.where(
            is_end, unpack_wide(text_low[5 * eighth : 6 * eighth], loan.shape[1]), loan[cut:]
        )
        back = outer(given)
        text_sums, text_others, start = [], [], 0

        def add_text(*parts):
            rows = sum(part.shape[0] for part in parts)
            part = jnp.concatenate(parts) if len(parts) > 1 else parts[0]
            part = after(part, *text_sums)
            own = lax.optimization_barrier(text_part[start : start + rows] + part.astype(jnp.float32))
            text_sums.append(own)
            text_others.append(inner(own.astype(jnp.bfloat16)))
            return start + rows

        start = add_text(unpack(outer_2k[:, cut:], 1), unpack(outer_3v, 2))
        root = jnp.sqrt((square_sum + inner(square_sum)) / DT + 1e-06)
        state = fold(query_kept, [kept(outer_2k, outer_2v, 0, END), kept(inner_2k, inner_2v, 0, MIDDLE)], state)
        rest = fold(query_kept, [kept(outer_3k, outer_3v, 0, END)], state, True)[0]
        mixed = [loan[:cut], back, rest]
        mixed_check = END
    else:
        mixed = [self_line(info, line_check, query_self, key_self, value_self, heads, seq_size, right, left)]
        mixed_check = None
        text_part, square_part = text_parts(text_memory, text_gain, text_weight)
        texts = [text_line(text_part, square_part, place, seq_size, right, left)]

    if paired:
        gain_two = jnp.stack([cross_gain, swap(cross_gain, 2)])
        gain_all = jnp.concatenate([gain_two, swap(gain_two, 1)]).reshape(1, -1)
        overs, spots = [], []
        for start_row, rows in chunks:
            spot = (mixed_check, start_row, rows, out_weight, tensor_size)
            spots.append(spot)
            sent = swap(project(info, mixed, *spot, ORDER + 1, 1), 1)
            own = project(info, mixed, *spot, ORDER + 3, 1)
            sent = after(sent, *overs)
            overs.append((own.astype(jnp.float32) + sent.astype(jnp.float32)).astype(jnp.bfloat16))
        sents = [swap(project(info, mixed, *spot, ORDER, 1), 1) for spot in spots]
        mines = [project(info, mixed, *spot, ORDER + 2, 1) for spot in spots]
        others = [swap(x, 2) for x in overs]
    else:
        gain_all = lax.all_gather(cross_gain, "tensor", axis=0, tiled=True).reshape(1, -1)
        partials = [
            project(info, mixed, mixed_check, start_row, rows, out_weight, tensor_size, ORDER, tensor_size)
            for start_row, rows in chunks
        ]
    if four:
        start = add_text(unpack(outer_3k, 2), wide_unpack(back, eighth))
        texts, row = [], 0
        for n in range(3):
            own, other = text_sums[n], text_others[n]
            share = root[row : row + own.shape[0]]
            row += own.shape[0]
            total = ((own + other.astype(jnp.float32)) / share[:, None]).astype(jnp.bfloat16)
            given = jnp.where(is_end, text_low[5 * eighth :], total) if n == 0 else total
            taken = outer(given)
            texts.append(jnp.where(is_end, taken, total))
            if n == 0:
                add_text(taken[eighth:])
    out, residuals = None, []
    for n, (start_row, rows) in enumerate(chunks):
        video = video_states[start_row : start_row + rows].astype(jnp.float32)
        if paired:
            residual = (
                video
                + mines[n].astype(jnp.float32)
                + sents[n].astype(jnp.float32)
                + after(others[n], *residuals).astype(jnp.float32)
            ).astype(jnp.bfloat16)
            across = swap(residual, 2)
            parts = [residual, across, swap(residual, 1), swap(across, 1)]
            base = ORDER + 2
        else:
            summed = lax.psum_scatter(partials[n], "tensor", scatter_dimension=1, tiled=True)
            residual = (video + summed.astype(jnp.float32)).astype(jnp.bfloat16)
            gathered = lax.all_gather(residual, "tensor", axis=1, tiled=True)
            parts = [gathered[:, m * piece : (m + 1) * piece] for m in range(tensor_size)]
            base = ORDER
        residuals.append(residual)
        soon = [m for m in range(tensor_size) if m % 2 == 0]
        later = [m for m in range(tensor_size) if m % 2 == 1]
        if n == 0:
            gained = gain_query(info, base, tensor_size, gain_all, query_weight)
        first = early_query(info, base, soon, [parts[m] for m in soon], gain_all, query_weight)
        sources = [*(parts[m] for m in later), gain_all, query_weight, *first, gained]
        if n < len(chunks) - 1:
            sources = [cross_query(info, base, later, sources, local_width)]
        spot = (local_width, start_row, local_rows, out)
        out = cross(info, base, LIMIT, texts, later, sources, *spot)
    return (jnp.concatenate(residuals), out)


def solution(mesh):
    in_specs = (
        P(("groups", "seq"), "tensor"),
        P(("groups", "seq"), "tensor"),
        P(("groups", "seq"), "tensor"),
        P(("groups", "seq"), "tensor"),
        P("tensor", None),
        P("tensor"),
        P(None, "tensor"),
        P("groups", "seq"),
        P("seq"),
        P("seq", None, "tensor"),
        P("groups"),
    )
    out_specs = (P(("groups", "seq"), "tensor"), P(("groups", "seq"), "tensor"))

    def body(*args):
        return shards(mesh.shape["seq"], mesh.shape["tensor"], *args)

    return jax.shard_map(body, mesh=mesh, in_specs=in_specs, out_specs=out_specs, check_vma=False)
```
